256 devices in a mesh: outer: 32 (over x, y, core), inner: 8 (over z).
Axes of the slice: x: 4, y: 4, z: 8, core: 2. Of those that a mesh axis runs over, the one named last changes fastest.
Arguments:
- queries: bfloat16 [32768, 5120], P(('outer', 'inner')), may hold values from -100 to 100
- key_values: bfloat16 [32768, 2048], P(('outer', 'inner')), may hold values from -64 to 64
- doc_lengths: int32 [32, 8], P('outer'), may hold values from 1 to 512, 1024 in all within a row
- pairing: int32 [32], replicated, may hold values from 0 to 31, as said below
- swap_ids: int32 [32, 8, 2], P('outer', 'inner'), may hold values from 0 to 3, as said below
- dest: int32 [32768, 1], P(('outer', 'inner')), may hold values from 0 to 7; in each aligned block of 128 rows (0 to 127, 128 to 255, ...) at most 32 rows name the same one
- gain: float32 [5120], replicated, may hold values from 0.1 to 1.9
Outputs:
- normed: bfloat16 [65536, 5120], P(('outer', 'inner'))
The draws below stay inside these ranges and needn't reach their ends.
Inputs may be any that keep to these rules, and one draw needn't show every extreme that they name: pairing[g] = g XOR m for one m of 1 to 31 in each draw, so pairing[pairing[g]] = g. Each device's listed numbers are distinct and increasing, and swap_ids[pairing[g]] = swap_ids[g]. `dest`: the rows of one device name each destination at most 32 times.
All inputs are finite; a program needn't handle non-finite values.
Results may differ from the reference program's by a relative error of at most 0.0059.
Values may be sent and summed in bfloat16 or wider, within the bound.
A program may use at most 128 MiB of HBM per device.

```python
import math
import jax
import jax.numpy as jnp
import numpy as np
from jax import lax

QUERY_HEADS = 40
KEY_VALUE_HEADS = 8
HEAD_SIZE = 128
TOK_DEV = 128
BLK = 32
NSWAP = 2
NDOCS = 8
GROUP = 1024
CAP = 32
TOKEN_TOTAL = 32768
N_OUTER = 32
N_INNER = 8


def pair_mask(key):
    return jax.random.randint(jax.random.fold_in(key, 11), (), 1, N_OUTER, dtype=jnp.int32)


def draw_pairing(key, part):
    mask_bits = pair_mask(key)
    return jnp.bitwise_xor(jnp.arange(N_OUTER, dtype=jnp.int32), mask_bits).astype(jnp.int32)


def draw_swap_ids(key, part):
    mask_bits = pair_mask(key)
    n_blocks = TOK_DEV // BLK
    scores = jax.random.randint(jax.random.fold_in(key, 12), (N_OUTER, N_INNER, n_blocks), 0, 1 << 20, dtype=jnp.int32)
    scores = scores * n_blocks + jnp.arange(n_blocks, dtype=jnp.int32)
    order = jnp.argsort(scores, axis=-1, stable=True)[:, :, :NSWAP]
    order = jnp.sort(order, axis=-1).astype(jnp.int32)
    seq_ids = jnp.arange(N_OUTER, dtype=jnp.int32)
    lower = jnp.minimum(seq_ids, jnp.bitwise_xor(seq_ids, mask_bits))
    return order[lower].astype(jnp.int32)


def key_rows(key):
    return jax.random.truncated_normal(jax.random.fold_in(key, 21), -4.0, 4.0, (TOKEN_TOTAL, KEY_VALUE_HEADS, HEAD_SIZE), jnp.float32)


def draw_key_values(key, part):
    key_matrix = key_rows(key)
    base_offset = jax.random.truncated_normal(jax.random.fold_in(key, 23), -4.0, 4.0, (TOKEN_TOTAL, KEY_VALUE_HEADS, HEAD_SIZE), jnp.float32)
    row_scale = jnp.exp(jax.random.uniform(jax.random.fold_in(key, 25), (TOKEN_TOTAL, 1, 1), jnp.float32, jnp.log(0.5), jnp.log(5.0)))
    column_scale = jnp.exp(jax.random.uniform(jax.random.fold_in(key, 26), (1, KEY_VALUE_HEADS, HEAD_SIZE), jnp.float32, jnp.log(0.3), jnp.log(3.0)))
    value_matrix = base_offset * row_scale * column_scale
    return jnp.stack([key_matrix, value_matrix], axis=2).reshape(TOKEN_TOTAL, KEY_VALUE_HEADS * 2 * HEAD_SIZE).astype(jnp.bfloat16)


def draw_queries(key, part):
    portion_each = QUERY_HEADS // KEY_VALUE_HEADS
    base_offset = jax.random.truncated_normal(jax.random.fold_in(key, 31), -4.0, 4.0, (TOKEN_TOTAL, KEY_VALUE_HEADS, portion_each, HEAD_SIZE), jnp.float32)
    return base_offset.reshape(TOKEN_TOTAL, QUERY_HEADS * HEAD_SIZE).astype(jnp.bfloat16)


def length_profile(number_of, total, most, slope):
    loads = [(1 << 20) // math.isqrt(grade ** slope) + 1 for grade in range(2, number_of + 1)]
    spare, given = total - most - (number_of - 1), [1] * (number_of - 1)
    while spare > 0:
        candidates = [i for i in range(number_of - 1) if given[i] < most]
        mass, remaining = sum([loads[i] for i in candidates]), spare
        for i in candidates:
            addition = min(most - given[i], max(1, remaining * loads[i] // mass), spare)
            given[i] = given[i] + addition
            spare = spare - addition
    return np.array([most] + given)


def uneven_parts(key, number_of, total, bound, skew):
    if number_of == 2:
        one = jax.random.randint(key, (), max(1, total - bound), min(bound, total - 1) + 1)
        return jnp.stack([one, total - one])
    sizes = jnp.asarray(length_profile(number_of, total, bound, skew), jnp.int32)
    pairs = (number_of - 1) // 2
    source_of, taker = sizes[1:1 + 2 * pairs:2], sizes[2:2 + 2 * pairs:2]
    slack = jnp.minimum(source_of - 1, bound - taker)
    passed = jax.random.randint(jax.random.fold_in(key, 1), (pairs,), 0, 1 << 20) % (slack + 1)
    sizes = sizes.at[1:1 + 2 * pairs:2].set(source_of - passed).at[2:2 + 2 * pairs:2].set(taker + passed)
    return sizes[jax.random.permutation(jax.random.fold_in(key, 2), number_of)]


def deal_out(key, own, number, rows, number_of, top, most, skew):
    order = jax.random.permutation(key, number_of)
    crowded, usual = shares(number_of, rows * top, most, skew, True), shares(number_of, rows * top, most, skew, False)
    places = jnp.arange(number_of)

    def named(sizes, turn):
        used = int((sizes > 0).sum())
        fixed = max(1, used // 4)
        passed = fixed + (places - fixed + turn * (used - fixed)) % max(1, number_of - fixed)
        return jnp.zeros((number_of,), jnp.int32).at[order[jnp.where(places < fixed, places, passed)]].set(jnp.asarray(sizes, jnp.int32))

    sizes = jnp.where(number % 4 == 0, named(crowded, number // 4), named(usual, number - number // 4 - 1))
    mixed = jax.random.permutation(jax.random.fold_in(own, 3), number_of)
    source_of, taker = mixed[0:number_of // 2 * 2:2], mixed[1:number_of // 2 * 2:2]
    room = jnp.minimum(sizes[source_of] - 1, most - sizes[taker]) // 2
    room = jnp.where((source_of == order[0]) | (taker == order[0]) | (sizes[taker] == 0), 0, jnp.maximum(room, 0))
    passed = jax.random.randint(jax.random.fold_in(own, 4), (number_of // 2,), 0, 1 << 20) % (room + 1)
    sizes = sizes.at[source_of].add(-passed).at[taker].add(passed)
    members = jnp.searchsorted(jnp.cumsum(sizes), jnp.arange(rows * top), side="right").astype(jnp.int32)
    listing = members.reshape(top, rows).T
    listing = listing[jax.random.permutation(jax.random.fold_in(own, 1), rows)]
    turn = jax.random.randint(jax.random.fold_in(own, 2), (rows, 1), 0, top)
    return jnp.take_along_axis(listing, (jnp.arange(top)[None, :] + turn) % top, axis=1)


def shares(count, total, bound, skew, full):
    portions = [(1 << 20) // math.isqrt(rank ** skew) + 1 for rank in range(1, count + 1)]
    largest = bound if full else min(bound, max(-(-total // count), total * portions[0] // sum(portions)))
    least = 1 if total - largest >= count - 1 else 0
    given, spare = [largest] + [least] * (count - 1), total - largest - least * (count - 1)
    while spare > 0:
        movable = [i for i in range(1, count) if given[i] < largest] or [i for i in range(1, count) if given[i] < bound]
        pool, remaining = sum([portions[i] for i in movable]), spare
        for i in movable:
            addition = min(bound - given[i], max(1, remaining * portions[i] // pool), spare)
            given[i] = given[i] + addition
            spare = spare - addition
    return np.array(given)


def setup_inputs(seed: int = 0) -> dict:
    arg_keys = jax.random.split(jax.random.key(seed), 8)
    queries = draw_queries(jax.random.fold_in(arg_keys[7], 71), 0)
    key_values = draw_key_values(jax.random.fold_in(arg_keys[7], 71), 0)
    doc_lengths = jax.vmap(lambda own: uneven_parts(own, NDOCS, GROUP, GROUP // 2, 2))(jax.random.split(arg_keys[2], N_OUTER)).reshape((N_OUTER, NDOCS)).astype(jnp.int32)
    pairing = draw_pairing(jax.random.fold_in(arg_keys[7], 71), 0)
    swap_ids = draw_swap_ids(jax.random.fold_in(arg_keys[7], 71), 0)
    dest_keys = jax.random.split(jax.random.fold_in(arg_keys[5], 1), TOKEN_TOTAL // TOK_DEV)
    dest_turns = jax.random.permutation(jax.random.fold_in(arg_keys[5], 3), TOKEN_TOTAL // TOK_DEV)
    dest = jax.vmap(lambda own, number: deal_out(jax.random.fold_in(arg_keys[5], 2), own, number, TOK_DEV, N_INNER, 1, CAP, 2))(dest_keys, dest_turns).reshape((TOKEN_TOTAL, 1))
    gain = jnp.clip(1.0 + 0.18 * jax.random.normal(arg_keys[6], (QUERY_HEADS * HEAD_SIZE,), jnp.float32), 0.1, 1.9)
    return {"queries": queries, "key_values": key_values, "doc_lengths": doc_lengths, "pairing": pairing, "swap_ids": swap_ids, "dest": dest, "gain": gain}


def doc_index(positions, lengths):
    ends = jnp.cumsum(lengths)
    return lax.optimization_barrier(jnp.sum((positions[:, None] >= ends[None, :]).astype(jnp.int32), axis=1))

def normalize(row_list, gain):
    value_matrix = row_list.astype(jnp.float32)
    factor = lax.rsqrt(lax.optimization_barrier(jnp.mean(value_matrix * value_matrix, axis=-1, keepdims=True)) + 1e-06)
    return (value_matrix * factor * gain).astype(jnp.bfloat16)

def reference(queries, key_values, doc_lengths, pairing, swap_ids, dest, gain):
    width = QUERY_HEADS * HEAD_SIZE
    key_value_width = KEY_VALUE_HEADS * 2 * HEAD_SIZE
    n_blocks = TOK_DEV // BLK
    grouped_row_list = N_INNER * TOK_DEV
    portion_each = QUERY_HEADS // KEY_VALUE_HEADS
    scale = 1.0 / math.sqrt(HEAD_SIZE)
    q_groups = queries.reshape(N_OUTER, N_INNER, n_blocks, BLK, width)
    kv_groups = key_values.reshape(N_OUTER, N_INNER, n_blocks, BLK, key_value_width)
    dest_groups = dest[:, 0].reshape(N_OUTER, N_INNER, TOK_DEV)
    positions = jnp.arange(grouped_row_list, dtype=jnp.int32)
    q_block = min(256, grouped_row_list)
    block_ids = jnp.arange(n_blocks, dtype=jnp.int32)
    inner_ids = jnp.arange(N_INNER, dtype=jnp.int32)

    def one_group(g):
        partner = pairing[g]
        listed = jnp.any(swap_ids[g][:, :, None] == block_ids[None, None, :], axis=1)
        chosen = listed[:, :, None, None]
        query_sequence = jnp.where(chosen, q_groups[partner], q_groups[g]).reshape(grouped_row_list, width)
        key_value_sequence = jnp.where(chosen, kv_groups[partner], kv_groups[g]).reshape(grouped_row_list, key_value_width)
        docs = doc_index(positions, doc_lengths[g])
        query_4 = query_sequence.reshape(grouped_row_list, KEY_VALUE_HEADS, portion_each, HEAD_SIZE).astype(jnp.float32)
        key_value_4 = key_value_sequence.reshape(grouped_row_list, KEY_VALUE_HEADS, 2, HEAD_SIZE).astype(jnp.float32)
        key_matrix = key_value_4[:, :, 0]
        value_matrix = key_value_4[:, :, 1]

        def one_block(index):
            start = index * q_block
            q_blk = lax.dynamic_slice_in_dim(query_4, start, q_block, 0)
            q_pos = start + jnp.arange(q_block, dtype=jnp.int32)
            q_doc = lax.dynamic_slice_in_dim(docs, start, q_block, 0)
            scores = jnp.einsum('qkgd,rkd->kgqr', q_blk, key_matrix) * scale
            allowed = (positions[None, :] <= q_pos[:, None]) & (docs[None, :] == q_doc[:, None])
            scores = jnp.where(allowed, scores, -1e+30)
            top = lax.optimization_barrier(jnp.max(scores, axis=-1, keepdims=True))
            expo = jnp.where(allowed, jnp.exp(scores - top), 0.0)
            total = lax.optimization_barrier(jnp.sum(expo, axis=-1))
            weights = lax.optimization_barrier(expo.astype(jnp.bfloat16)).astype(jnp.float32)
            numer = jnp.einsum('kgqr,rkd->qkgd', weights, value_matrix)
            result = numer / jnp.transpose(total, (2, 0, 1))[..., None]
            return result.astype(jnp.bfloat16).reshape(q_block, width)
        attn = lax.map(one_block, jnp.arange(grouped_row_list // q_block, dtype=jnp.int32)).reshape(grouped_row_list, width)
        normed = normalize(attn, gain)
        dest_g = dest_groups[g]
        onehot = (dest_g[:, :, None] == inner_ids[None, None, :]).astype(jnp.int32)
        rank = lax.optimization_barrier(jnp.sum(jnp.cumsum(onehot, axis=1) * onehot, axis=2)) - 1
        place = ((dest_g * N_INNER + inner_ids[:, None]) * CAP + rank).reshape(grouped_row_list).astype(jnp.int32)
        return jnp.zeros((N_INNER * N_INNER * CAP, width), jnp.bfloat16).at[place].set(normed)
    result = lax.map(one_group, jnp.arange(N_OUTER, dtype=jnp.int32))
    return result.reshape(N_OUTER * N_INNER * N_INNER * CAP, width)
```

```python
import math

import jax
import jax.numpy as jnp
from jax import lax
from jax.experimental import pallas as pl
from jax.experimental.pallas import tpu as pltpu
from jax.sharding import PartitionSpec as P

HEADS = 40
KVH = 8
D = 128
BLK = 32
PER = HEADS // KVH
WQ = PER * D
T = 128
N = 8
REACH = 4
SLOTS = REACH + 1
CAP = 32
KEYS = SLOTS * T
NEG = -1e30
WIDTH = HEADS * D
MESH = pl.DeviceIdType.MESH


def fused(
    ids, lens, q, kv, rq, rkv, drow, dcol, gain, out,
    kvbuf, sendbuf, recvbuf, bias, perm, kv_ss, kv_rs, a_ss, a_rs,
):
    me = lax.axis_index("inner")

    barrier = pltpu.get_barrier_semaphore()
    for k in range(1, N):
        pl.semaphore_signal(
            barrier, inc=1, device_id={"inner": lax.rem(me + k, N)}, device_id_type=MESH
        )

    id0, id1 = ids[0], ids[1]

    def chosen(block, own, first, second):
        return jnp.where(id0 == block, first, jnp.where(id1 == block, second, own))

    for h in range(KVH):
        cols = slice(h * 2 * D, (h + 1) * 2 * D)
        for b in range(T // BLK):
            rows = slice(b * BLK, (b + 1) * BLK)
            kvbuf[0, h, rows, :] = chosen(b, kv[rows, cols], rkv[0, :, cols], rkv[1, :, cols])
    for s in range(1, SLOTS):

        @pl.when(me < s)
        def _():
            kvbuf[s] = jnp.zeros(kvbuf.shape[1:], kvbuf.dtype)

    qpos = me * T + lax.broadcasted_iota(jnp.int32, (T, KEYS), 0)
    lane = lax.broadcasted_iota(jnp.int32, (T, KEYS), 1)
    kpos = (me - lane // T) * T + lax.rem(lane, T)
    start = jnp.zeros((T, KEYS), jnp.int32)
    end = lens[0, 0]
    for k in range(1, 9):
        start = jnp.where(qpos >= end, jnp.maximum(start, end), start)
        if k < 8:
            end = end + lens[0, k]
    bias[...] = jnp.where((kpos <= qpos) & (kpos >= start), 0.0, NEG)

    first = lax.broadcasted_iota(jnp.int32, (T, T), 0)
    second = lax.broadcasted_iota(jnp.int32, (T, T), 1)
    same = (dcol[...] == drow[...]) & (first < second)
    rank = jnp.sum(same.astype(jnp.int32), axis=0, keepdims=True)
    place = drow[...] * CAP + rank
    slot = lax.broadcasted_iota(jnp.int32, (N * CAP, T), 0)
    perm[...] = (slot == place).astype(jnp.float32).astype(jnp.bfloat16)

    pl.semaphore_wait(barrier, N - 1)

    def kv_copy(s, h):
        return pltpu.make_async_remote_copy(
            src_ref=kvbuf.at[s, h],
            dst_ref=kvbuf.at[s + 1, h],
            send_sem=kv_ss.at[s, h],
            recv_sem=kv_rs.at[s + 1, h],
            device_id={"inner": lax.rem(me + 1, N)},
            device_id_type=MESH,
        )

    def row_copy(h, k):
        to = lax.rem(me + k, N)
        return pltpu.make_async_remote_copy(
            src_ref=sendbuf.at[h, to],
            dst_ref=recvbuf.at[h, me],
            send_sem=a_ss.at[h, k],
            recv_sem=a_rs.at[h, k],
            device_id={"inner": to},
            device_id_type=MESH,
        )

    factor = math.log2(math.e) / math.sqrt(D)

    def attend(h):
        cols = pl.ds(pl.multiple_of(h * WQ, D), WQ)
        own, r0, r1 = q[:, cols], rq[0, :, cols], rq[1, :, cols]
        qh = jnp.concatenate(
            [chosen(b, own[b * BLK : (b + 1) * BLK], r0, r1) for b in range(T // BLK)], axis=0
        )
        keys = kvbuf[:, h, :, :D].reshape(KEYS, D)
        values = kvbuf[:, h, :, D:].reshape(KEYS, D)
        parts = []
        for g in range(PER):
            s = lax.dot_general(
                qh[:, g * D : (g + 1) * D],
                keys,
                (((1,), (1,)), ((), ())),
                preferred_element_type=jnp.float32,
            )
            s = s + bias[...]
            expo = jnp.exp2((s - jnp.max(s, axis=1, keepdims=True)) * factor)
            total = jnp.sum(expo, axis=1, keepdims=True)
            acc = jnp.dot(expo.astype(jnp.bfloat16), values, preferred_element_type=jnp.float32)
            parts.append((acc * (1.0 / total)).astype(jnp.bfloat16))
        attn = jnp.concatenate(parts, axis=1)
        placed = jnp.dot(perm[...], attn, preferred_element_type=jnp.float32)
        sendbuf[h] = placed.astype(jnp.bfloat16).reshape(N, CAP, WQ)
        recvbuf[h, me] = sendbuf[h, me]
        for k in (4, 3, 5, 2, 6, 1, 7):
            row_copy(h, k).start()

    @pl.loop(0, KVH + REACH)
    def _(t):
        for s in range(REACH):
            h = t - s

            @pl.when((h >= 0) & (h < KVH))
            def _():
                if s > 0:

                    @pl.when(me >= s)
                    def _():
                        kv_copy(s - 1, h).wait_recv()

                @pl.when((me >= s) & (me < N - 1))
                def _():
                    kv_copy(s, h).start()

        h = t - REACH

        @pl.when(h >= 0)
        def _():
            @pl.when(me >= REACH)
            def _():
                kv_copy(REACH - 1, h).wait_recv()

            attend(h)

    @pl.loop(0, KVH)
    def _(h):
        for k in range(1, N):
            row_copy(h, k).wait_recv()

    @pl.loop(0, N)
    def _(i):
        square = jnp.zeros((CAP, WQ), jnp.float32)
        for h in range(KVH):
            x = recvbuf[h, i].astype(jnp.float32)
            square = square + x * x
        mean = jnp.sum(square, axis=1, keepdims=True) * (1.0 / WIDTH)
        norm = lax.rsqrt(mean + 1e-06)
        rows = pl.ds(pl.multiple_of(i * CAP, CAP), CAP)
        for h in range(KVH):
            cols = slice(h * WQ, (h + 1) * WQ)
            x = recvbuf[h, i].astype(jnp.float32)
            out[rows, cols] = (x * norm * gain[:, cols]).astype(jnp.bfloat16)

    @pl.loop(0, KVH)
    def _(h):
        for k in range(1, N):
            row_copy(h, k).wait_send()
        for s in range(REACH):

            @pl.when((me >= s) & (me < N - 1))
            def _():
                kv_copy(s, h).wait_send()


def exchange(queries, key_values, pairing, listed):
    def block(x, k):
        return lax.dynamic_slice(x, (listed[k] * BLK, 0), (BLK, x.shape[1]))

    q_out = jnp.stack([block(queries, 0), block(queries, 1)])
    kv_out = jnp.stack([block(key_values, 0), block(key_values, 1)])
    size = lax.axis_size("outer")

    def branch(mask):
        pairs = [(g, g ^ mask) for g in range(size)]
        return lambda a, b: (lax.ppermute(a, "outer", pairs), lax.ppermute(b, "outer", pairs))

    return lax.switch(pairing[0] - 1, [branch(m) for m in range(1, size)], q_out, kv_out)


def shards(queries, key_values, doc_lengths, pairing, swap_ids, dest, gain):
    listed = swap_ids[0, 0]
    rq, rkv = exchange(queries, key_values, pairing, listed)
    vmem = pl.BlockSpec(memory_space=pltpu.VMEM)
    smem = pl.BlockSpec(memory_space=pltpu.SMEM)
    return pl.pallas_call(
        fused,
        name="attend_and_route",
        out_shape=jax.ShapeDtypeStruct((N * CAP, WIDTH), jnp.bfloat16),
        in_specs=[smem, smem] + [vmem] * 7,
        out_specs=vmem,
        scratch_shapes=[
            pltpu.VMEM((SLOTS, KVH, T, 2 * D), jnp.bfloat16),
            pltpu.VMEM((KVH, N, CAP, WQ), jnp.bfloat16),
            pltpu.VMEM((KVH, N, CAP, WQ), jnp.bfloat16),
            pltpu.VMEM((T, KEYS), jnp.float32),
            pltpu.VMEM((N * CAP, T), jnp.bfloat16),
            pltpu.SemaphoreType.DMA((SLOTS, KVH)),
            pltpu.SemaphoreType.DMA((SLOTS, KVH)),
            pltpu.SemaphoreType.DMA((KVH, N)),
            pltpu.SemaphoreType.DMA((KVH, N)),
        ],
        compiler_params=pltpu.CompilerParams(
            collective_id=0, has_side_effects=True, vmem_limit_bytes=48 << 20
        ),
    )(
        listed, doc_lengths, queries, key_values, rq, rkv,
        dest.reshape(1, T), dest, gain.reshape(1, WIDTH),
    )


def solution(mesh):
    return jax.shard_map(
        shards,
        mesh=mesh,
        in_specs=(
            P(("outer", "inner"), None),
            P(("outer", "inner"), None),
            P("outer", None),
            P(),
            P("outer", "inner", None),
            P(("outer", "inner"), None),
            P(),
        ),
        out_specs=P(("outer", "inner"), None),
        check_vma=False,
    )
```

```python
import math

import jax
import jax.numpy as jnp
from jax import lax
from jax.experimental import pallas as pl
from jax.experimental.pallas import tpu as pltpu
from jax.sharding import PartitionSpec as P

HEADS = 40
KVH = 8
D = 128
BLK = 32
PER = HEADS // KVH
WQ = PER * D
T = 128
N = 8
REACH = 4
SLOTS = REACH + 1
CAP = 32
KEYS = SLOTS * T
NEG = -1e30
WIDTH = HEADS * D
MESH = pl.DeviceIdType.MESH


def fused(
    ids, lens, pair, q, kv, drow, gain, out,
    kvbuf, sendbuf, recvbuf, bias, perm,
    kv_own, kv_core, kv_mid, kv_in1, kv_far, kv_in2,
    q_own, q_core, q_mid, q_in1, q_far, q_in2,
    kv_ss, kv_rs, a_ss, a_rs, core_ss, core_rs, one_ss, one_rs, two_ss, two_rs,
):
    me = lax.axis_index("inner")
    seq = lax.axis_index("outer")
    core, y, x = lax.rem(seq, 2), lax.rem(seq // 2, 4), seq // 8

    def flipped(i, k):
        if k == 1:
            return i + 1 - 2 * lax.rem(i, 2)
        return i + 2 - 4 * (i // 2) if k == 2 else 3 - i

    other_core = seq + 1 - 2 * core
    peers = {
        "y": [seq + 2 * (flipped(y, k) - y) for k in (1, 2, 3)],
        "x": [seq + 8 * (flipped(x, k) - x) for k in (1, 2, 3)],
    }

    barrier = pltpu.get_barrier_semaphore()
    greet = [{"inner": lax.rem(me + k, N)} for k in range(1, N)]
    greet += [{"outer": g} for g in (other_core, *peers["y"], *peers["x"])]
    for device in greet:
        pl.semaphore_signal(barrier, inc=1, device_id=device, device_id_type=MESH)

    id0, id1 = ids[0], ids[1]
    mask = pair[0]
    bits = {"core": lax.rem(mask, 2), "y": lax.rem(lax.div(mask, 2), 4), "x": lax.div(mask, 8)}

    def chosen(block, own, first, second):
        return jnp.where(id0 == block, first, jnp.where(id1 == block, second, own))

    kinds = (
        (kv, 2 * D, kv_own, kv_core, kv_mid, kv_in1, kv_far, kv_in2),
        (q, WQ, q_own, q_core, q_mid, q_in1, q_far, q_in2),
    )
    routes = (("y", "x"), ("x", "y"))

    def core_copy(kind, h):
        _, _, mine, theirs, *_ = kinds[kind]
        return pltpu.make_async_remote_copy(
            src_ref=mine.at[h],
            dst_ref=theirs.at[h],
            send_sem=core_ss.at[kind, h],
            recv_sem=core_rs.at[kind, h],
            device_id={"outer": other_core},
            device_id_type=MESH,
        )

    def axis_copies(source, target, ss, rs, kind, h, b, axis):
        return [
            pltpu.make_async_remote_copy(
                src_ref=source.at[h, b],
                dst_ref=target.at[h, b, k],
                send_sem=ss.at[kind, h, b],
                recv_sem=rs.at[kind, h, b],
                device_id={"outer": peer},
                device_id_type=MESH,
            )
            for k, peer in enumerate(peers[axis])
        ]

    def all_three(target, sems, kind, h, b):
        whole = target.at[h, b]
        pltpu.make_async_copy(whole, whole, sems.at[kind, h, b]).wait()

    def picked(source, target, h, b, axis):
        v = bits[axis]
        value = source[h, b]
        for k in (1, 2, 3):
            value = jnp.where(v == k, target[h, b, k - 1], value)
        return value

    def swap_core(kind, h):
        ref, width, mine, *_ = kinds[kind]
        cols = pl.ds(pl.multiple_of(h * width, D), width)
        blocks = [ref[b * BLK : (b + 1) * BLK, cols] for b in range(T // BLK)]
        for b, listed in enumerate((id0, id1)):
            value = blocks[0]
            for block in range(1, T // BLK):
                value = jnp.where(listed == block, blocks[block], value)
            mine[h, b] = value
        core_copy(kind, h).start()

    def swap_one(kind, h):
        _, _, mine, theirs, mid, in1, _, _ = kinds[kind]
        core_copy(kind, h).wait_recv()
        mid[h] = jnp.where(bits["core"] == 1, theirs[h], mine[h])
        for b in (0, 1):
            for copy in axis_copies(mid, in1, one_ss, one_rs, kind, h, b, routes[b][0]):
                copy.start()

    def swap_two(kind, h):
        _, _, _, _, mid, in1, far, in2 = kinds[kind]
        for b in (0, 1):
            all_three(in1, one_rs, kind, h, b)
            far[h, b] = picked(mid, in1, h, b, routes[b][0])
            for copy in axis_copies(far, in2, two_ss, two_rs, kind, h, b, routes[b][1]):
                copy.start()

    def swapped(kind, h):
        _, _, _, _, _, _, far, in2 = kinds[kind]
        for b in (0, 1):
            all_three(in2, two_rs, kind, h, b)
        return [picked(far, in2, h, b, routes[b][1]) for b in (0, 1)]

    def tables():
        for s in range(1, SLOTS):

            @pl.when(me < s)
            def _():
                kvbuf[s] = jnp.zeros(kvbuf.shape[1:], kvbuf.dtype)

        qpos = me * T + lax.broadcasted_iota(jnp.int32, (T, KEYS), 0)
        lane = lax.broadcasted_iota(jnp.int32, (T, KEYS), 1)
        kpos = (me - lane // T) * T + lax.rem(lane, T)
        start = jnp.zeros((T, KEYS), jnp.int32)
        end = lens[0, 0]
        for k in range(1, 9):
            start = jnp.where(qpos >= end, jnp.maximum(start, end), start)
            if k < 8:
                end = end + lens[0, k]
        bias[...] = jnp.where((kpos <= qpos) & (kpos >= start), 0.0, NEG)

        first = lax.broadcasted_iota(jnp.int32, (T, T), 0)
        second = lax.broadcasted_iota(jnp.int32, (T, T), 1)
        row = drow[...].astype(jnp.float32)
        column = jnp.sum(jnp.where(first == second, row, 0.0), axis=1, keepdims=True)
        same = (column == row) & (first < second)
        rank = jnp.sum(same.astype(jnp.int32), axis=0, keepdims=True)
        place = drow[...] * CAP + rank
        slot = lax.broadcasted_iota(jnp.int32, (N * CAP, T), 0)
        perm[...] = (slot == place).astype(jnp.float32).astype(jnp.bfloat16)

    def kv_copy(s, h):
        return pltpu.make_async_remote_copy(
            src_ref=kvbuf.at[s, h],
            dst_ref=kvbuf.at[s + 1, h],
            send_sem=kv_ss.at[s, h],
            recv_sem=kv_rs.at[s + 1, h],
            device_id={"inner": lax.rem(me + 1, N)},
            device_id_type=MESH,
        )

    def row_copy(h, k):
        to = lax.rem(me + k, N)
        return pltpu.make_async_remote_copy(
            src_ref=sendbuf.at[h, to],
            dst_ref=recvbuf.at[h, me],
            send_sem=a_ss.at[h, k],
            recv_sem=a_rs.at[h, k],
            device_id={"inner": to},
            device_id_type=MESH,
        )

    def forward(s, h):
        if s > 0:

            @pl.when(me >= s)
            def _():
                kv_copy(s - 1, h).wait_recv()

        else:
            cols = pl.ds(pl.multiple_of(h * 2 * D, D), 2 * D)
            r0, r1 = swapped(0, h)
            for b in range(T // BLK):
                rows = slice(b * BLK, (b + 1) * BLK)
                kvbuf[0, h, rows, :] = chosen(b, kv[rows, cols], r0, r1)

        @pl.when((me >= s) & (me < N - 1))
        def _():
            kv_copy(s, h).start()

    factor = math.log2(math.e) / math.sqrt(D)

    def attend(h):
        @pl.when(me >= REACH)
        def _():
            kv_copy(REACH - 1, h).wait_recv()

        own = q[:, pl.ds(pl.multiple_of(h * WQ, D), WQ)]
        r0, r1 = swapped(1, h)
        qh = jnp.concatenate(
            [chosen(b, own[b * BLK : (b + 1) * BLK], r0, r1) for b in range(T // BLK)], axis=0
        )
        keys = kvbuf[:, h, :, :D].reshape(KEYS, D)
        values = kvbuf[:, h, :, D:].reshape(KEYS, D)
        parts = []
        for g in range(PER):
            s = lax.dot_general(
                qh[:, g * D : (g + 1) * D],
                keys,
                (((1,), (1,)), ((), ())),
                preferred_element_type=jnp.float32,
            )
            s = s + bias[...]
            expo = jnp.exp2((s - jnp.max(s, axis=1, keepdims=True)) * factor)
            total = jnp.sum(expo, axis=1, keepdims=True)
            acc = jnp.dot(expo.astype(jnp.bfloat16), values, preferred_element_type=jnp.float32)
            parts.append((acc * (1.0 / total)).astype(jnp.bfloat16))
        attn = jnp.concatenate(parts, axis=1)
        placed = jnp.dot(perm[...], attn, preferred_element_type=jnp.float32)
        sendbuf[h] = placed.astype(jnp.bfloat16).reshape(N, CAP, WQ)
        recvbuf[h, me] = sendbuf[h, me]
        for k in (4, 3, 5, 2, 6, 1, 7):
            row_copy(h, k).start()

    pl.semaphore_wait(barrier, len(greet))

    kv_lag = 3
    last = kv_lag + REACH
    stages = [(kv_lag + s, lambda h, s=s: forward(s, h)) for s in reversed(range(REACH))]
    stages += [(2, lambda h: swap_two(0, h)), (1, lambda h: swap_one(0, h))]
    stages += [(0, lambda h: swap_core(0, h))]
    stages += [(last - 1, lambda h: swap_two(1, h)), (last - 2, lambda h: swap_one(1, h))]
    stages += [(last - 3, lambda h: swap_core(1, h)), (last, attend)]

    @pl.loop(0, KVH + last)
    def _(t):
        for lag, stage in stages:
            h = t - lag

            @pl.when((h >= 0) & (h < KVH))
            def _():
                stage(h)

        @pl.when(t == 1)
        def _():
            tables()

    @pl.loop(0, KVH)
    def _(h):
        for k in range(1, N):
            row_copy(h, k).wait_recv()

    @pl.loop(0, N)
    def _(i):
        square = jnp.zeros((CAP, WQ), jnp.float32)
        for h in range(KVH):
            part = recvbuf[h, i].astype(jnp.float32)
            square = square + part * part
        mean = jnp.sum(square, axis=1, keepdims=True) * (1.0 / WIDTH)
        norm = lax.rsqrt(mean + 1e-06)
        rows = pl.ds(pl.multiple_of(i * CAP, CAP), CAP)
        for h in range(KVH):
            cols = slice(h * WQ, (h + 1) * WQ)
            part = recvbuf[h, i].astype(jnp.float32)
            out[rows, cols] = (part * norm * gain[:, cols]).astype(jnp.bfloat16)

    @pl.loop(0, KVH)
    def _(h):
        for k in range(1, N):
            row_copy(h, k).wait_send()
        for s in range(REACH):

            @pl.when((me >= s) & (me < N - 1))
            def _():
                kv_copy(s, h).wait_send()

        for kind in (0, 1):
            core_copy(kind, h).wait_send()
            for b in (0, 1):
                all_three(kinds[kind][5], one_ss, kind, h, b)
                all_three(kinds[kind][7], two_ss, kind, h, b)


def shards(queries, key_values, doc_lengths, pairing, swap_ids, dest, gain):
    listed = swap_ids[0, 0]
    vmem = pl.BlockSpec(memory_space=pltpu.VMEM)
    smem = pl.BlockSpec(memory_space=pltpu.SMEM)
    dma = pltpu.SemaphoreType.DMA

    def swap_buffers(width):
        shapes = [(KVH, 2), (KVH, 2), (KVH, 2), (KVH, 2, 3), (KVH, 2), (KVH, 2, 3)]
        return [pltpu.VMEM((*shape, BLK, width), jnp.bfloat16) for shape in shapes]

    return pl.pallas_call(
        fused,
        name="attend_and_route",
        out_shape=jax.ShapeDtypeStruct((N * CAP, WIDTH), jnp.bfloat16),
        in_specs=[smem] * 3 + [vmem] * 4,
        out_specs=vmem,
        scratch_shapes=[
            pltpu.VMEM((SLOTS, KVH, T, 2 * D), jnp.bfloat16),
            pltpu.VMEM((KVH, N, CAP, WQ), jnp.bfloat16),
            pltpu.VMEM((KVH, N, CAP, WQ), jnp.bfloat16),
            pltpu.VMEM((T, KEYS), jnp.float32),
            pltpu.VMEM((N * CAP, T), jnp.bfloat16),
            *swap_buffers(2 * D),
            *swap_buffers(WQ),
            *(dma((SLOTS, KVH)) for _ in range(2)),
            *(dma((KVH, N)) for _ in range(2)),
            *(dma((2, KVH)) for _ in range(2)),
            *(dma((2, KVH, 2)) for _ in range(4)),
        ],
        compiler_params=pltpu.CompilerParams(
            collective_id=0, has_side_effects=True, vmem_limit_bytes=48 << 20
        ),
    )(
        listed, doc_lengths, pairing, queries, key_values,
        dest.reshape(1, T), gain.reshape(1, WIDTH),
    )


def solution(mesh):
    return jax.shard_map(
        shards,
        mesh=mesh,
        in_specs=(
            P(("outer", "inner"), None),
            P(("outer", "inner"), None),
            P("outer", None),
            P(),
            P("outer", "inner", None),
            P(("outer", "inner"), None),
            P(),
        ),
        out_specs=P(("outer", "inner"), None),
        check_vma=False,
    )
```

```python
import math

import jax
import jax.numpy as jnp
from jax import lax
from jax.experimental import pallas as pl
from jax.experimental.pallas import tpu as pltpu
from jax.sharding import PartitionSpec as P

HEADS = 40
KVH = 8
D = 128
BLK = 32
PER = HEADS // KVH
WQ = PER * D
T = 128
N = 8
REACH = 4
SLOTS = REACH + 1
CAP = 32
KEYS = SLOTS * T
NEG = -1e30
DIRECT = (3, 5, 2, 6, 1, 7)
WIDTH = HEADS * D
MESH = pl.DeviceIdType.MESH


def fused(
    ids_hbm, lens_hbm, pair_hbm, q_hbm, kv_hbm, drow_hbm, gain_hbm, out,
    ids, lens, pair, q, kv, drow, gain, load_s,
    kvbuf, sendbuf, recvbuf, relay, bias, perm,
    kv_own, kv_core, kv_mid, kv_in1, kv_far, kv_in2,
    q_own, q_core, q_mid, q_in1, q_far, q_in2,
    kv_ss, kv_rs, a_ss, a_rs, r_ss, r_rs, core_ss, core_rs, one_ss, one_rs, two_ss, two_rs,
):
    me = lax.axis_index("inner")
    seq = lax.axis_index("outer")
    core, y, x = lax.rem(seq, 2), lax.rem(seq // 2, 4), seq // 8

    def flipped(i, k):
        if k == 1:
            return i + 1 - 2 * lax.rem(i, 2)
        return i + 2 - 4 * (i // 2) if k == 2 else 3 - i

    other_core = seq + 1 - 2 * core
    peers = {
        "y": [seq + 2 * (flipped(y, k) - y) for k in (1, 2, 3)],
        "x": [seq + 8 * (flipped(x, k) - x) for k in (1, 2, 3)],
    }

    sources = (ids_hbm, pair_hbm, kv_hbm, q_hbm, drow_hbm, lens_hbm, gain_hbm)
    targets = (ids, pair, kv, q, drow, lens, gain)
    loads = [
        pltpu.make_async_copy(a, b, load_s.at[i]) for i, (a, b) in enumerate(zip(sources, targets))
    ]
    for load in loads:
        load.start()

    barrier = pltpu.get_barrier_semaphore()
    greet = [{"inner": lax.rem(me + k, N)} for k in range(1, N)]
    greet += [{"outer": g} for g in (other_core, *peers["y"], *peers["x"])]
    for device in greet:
        pl.semaphore_signal(barrier, inc=1, device_id=device, device_id_type=MESH)

    for load in loads:
        load.wait()
    id0, id1 = ids[0], ids[1]
    mask = pair[0]
    bits = {"core": lax.rem(mask, 2), "y": lax.rem(lax.div(mask, 2), 4), "x": lax.div(mask, 8)}

    def chosen(block, own, first, second):
        return jnp.where(id0 == block, first, jnp.where(id1 == block, second, own))

    kinds = (
        (kv, 2 * D, kv_own, kv_core, kv_mid, kv_in1, kv_far, kv_in2),
        (q, WQ, q_own, q_core, q_mid, q_in1, q_far, q_in2),
    )
    routes = (("y", "x"), ("x", "y"))

    def core_copy(kind, h):
        _, _, mine, theirs, *_ = kinds[kind]
        return pltpu.make_async_remote_copy(
            src_ref=mine.at[h],
            dst_ref=theirs.at[h],
            send_sem=core_ss.at[kind, h],
            recv_sem=core_rs.at[kind, h],
            device_id={"outer": other_core},
            device_id_type=MESH,
        )

    def axis_copies(source, target, ss, rs, kind, h, b, axis):
        return [
            pltpu.make_async_remote_copy(
                src_ref=source.at[h, b],
                dst_ref=target.at[h, b, k],
                send_sem=ss.at[kind, h, b],
                recv_sem=rs.at[kind, h, b],
                device_id={"outer": peer},
                device_id_type=MESH,
            )
            for k, peer in enumerate(peers[axis])
        ]

    def all_three(target, sems, kind, h, b):
        whole = target.at[h, b]
        pltpu.make_async_copy(whole, whole, sems.at[kind, h, b]).wait()

    def picked(source, target, h, b, axis):
        v = bits[axis]
        value = source[h, b]
        for k in (1, 2, 3):
            value = jnp.where(v == k, target[h, b, k - 1], value)
        return value

    def swap_core(kind, h):
        ref, width, mine, *_ = kinds[kind]
        cols = pl.ds(pl.multiple_of(h * width, D), width)
        blocks = [ref[b * BLK : (b + 1) * BLK, cols] for b in range(T // BLK)]
        for b, listed in enumerate((id0, id1)):
            value = blocks[0]
            for block in range(1, T // BLK):
                value = jnp.where(listed == block, blocks[block], value)
            mine[h, b] = value
        core_copy(kind, h).start()

    def swap_one(kind, h):
        _, _, mine, theirs, mid, in1, _, _ = kinds[kind]
        core_copy(kind, h).wait_recv()
        mid[h] = jnp.where(bits["core"] == 1, theirs[h], mine[h])
        for b in (0, 1):
            for copy in axis_copies(mid, in1, one_ss, one_rs, kind, h, b, routes[b][0]):
                copy.start()

    def swap_two(kind, h):
        _, _, _, _, mid, in1, far, in2 = kinds[kind]
        for b in (0, 1):
            all_three(in1, one_rs, kind, h, b)
            far[h, b] = picked(mid, in1, h, b, routes[b][0])
            for copy in axis_copies(far, in2, two_ss, two_rs, kind, h, b, routes[b][1]):
                copy.start()

    def swapped(kind, h):
        _, _, _, _, _, _, far, in2 = kinds[kind]
        for b in (0, 1):
            all_three(in2, two_rs, kind, h, b)
        return [picked(far, in2, h, b, routes[b][1]) for b in (0, 1)]

    def tables():
        for s in range(1, SLOTS):

            @pl.when(me < s)
            def _():
                kvbuf[s] = jnp.zeros(kvbuf.shape[1:], kvbuf.dtype)

        qpos = me * T + lax.broadcasted_iota(jnp.int32, (T, KEYS), 0)
        lane = lax.broadcasted_iota(jnp.int32, (T, KEYS), 1)
        kpos = (me - lane // T) * T + lax.rem(lane, T)
        start = jnp.zeros((T, KEYS), jnp.int32)
        end = lens[0, 0]
        for k in range(1, 9):
            start = jnp.where(qpos >= end, jnp.maximum(start, end), start)
            if k < 8:
                end = end + lens[0, k]
        bias[...] = jnp.where((kpos <= qpos) & (kpos >= start), 0.0, NEG)

        first = lax.broadcasted_iota(jnp.int32, (T, T), 0)
        second = lax.broadcasted_iota(jnp.int32, (T, T), 1)
        row = drow[...].astype(jnp.float32)
        column = jnp.sum(jnp.where(first == second, row, 0.0), axis=1, keepdims=True)
        same = (column == row) & (first < second)
        rank = jnp.sum(same.astype(jnp.int32), axis=0, keepdims=True)
        place = drow[...] * CAP + rank
        slot = lax.broadcasted_iota(jnp.int32, (N * CAP, T), 0)
        perm[...] = (slot == place).astype(jnp.float32).astype(jnp.bfloat16)

    def kv_copy(s, h):
        return pltpu.make_async_remote_copy(
            src_ref=kvbuf.at[s, h],
            dst_ref=kvbuf.at[s + 1, h],
            send_sem=kv_ss.at[s, h],
            recv_sem=kv_rs.at[s + 1, h],
            device_id={"inner": lax.rem(me + 1, N)},
            device_id_type=MESH,
        )

    def row_copy(h, k):
        to = lax.rem(me + k, N)
        return pltpu.make_async_remote_copy(
            src_ref=sendbuf.at[h, to],
            dst_ref=recvbuf.at[h, me],
            send_sem=a_ss.at[h, k],
            recv_sem=a_rs.at[h, k],
            device_id={"inner": to},
            device_id_type=MESH,
        )

    def relay_in(h):
        return pltpu.make_async_remote_copy(
            src_ref=sendbuf.at[h, lax.rem(me + 4, N)],
            dst_ref=relay.at[h],
            send_sem=r_ss.at[0, h],
            recv_sem=r_rs.at[h],
            device_id={"inner": lax.rem(me + 6, N)},
            device_id_type=MESH,
        )

    def relay_out(h):
        return pltpu.make_async_remote_copy(
            src_ref=relay.at[h],
            dst_ref=recvbuf.at[h, lax.rem(me + 2, N)],
            send_sem=r_ss.at[1, h],
            recv_sem=a_rs.at[h, 4],
            device_id={"inner": lax.rem(me + 6, N)},
            device_id_type=MESH,
        )

    def pass_on(h):
        relay_in(h).wait_recv()
        relay_out(h).start()

    def forward(s, h):
        if s > 0:

            @pl.when(me >= s)
            def _():
                kv_copy(s - 1, h).wait_recv()

        else:
            cols = pl.ds(pl.multiple_of(h * 2 * D, D), 2 * D)
            r0, r1 = swapped(0, h)
            for b in range(T // BLK):
                rows = slice(b * BLK, (b + 1) * BLK)
                kvbuf[0, h, rows, :] = chosen(b, kv[rows, cols], r0, r1)

        @pl.when((me >= s) & (me < N - 1))
        def _():
            kv_copy(s, h).start()

    factor = math.log2(math.e) / math.sqrt(D)

    def attend(h):
        @pl.when(me >= REACH)
        def _():
            kv_copy(REACH - 1, h).wait_recv()

        own = q[:, pl.ds(pl.multiple_of(h * WQ, D), WQ)]
        r0, r1 = swapped(1, h)
        qh = jnp.concatenate(
            [chosen(b, own[b * BLK : (b + 1) * BLK], r0, r1) for b in range(T // BLK)], axis=0
        )
        keys = kvbuf[:, h, :, :D].reshape(KEYS, D)
        values = kvbuf[:, h, :, D:].reshape(KEYS, D)
        parts = []
        for g in range(PER):
            s = lax.dot_general(
                qh[:, g * D : (g + 1) * D],
                keys,
                (((1,), (1,)), ((), ())),
                preferred_element_type=jnp.float32,
            )
            s = s + bias[...]
            expo = jnp.exp2((s - jnp.max(s, axis=1, keepdims=True)) * factor)
            total = jnp.sum(expo, axis=1, keepdims=True)
            acc = jnp.dot(expo.astype(jnp.bfloat16), values, preferred_element_type=jnp.float32)
            parts.append((acc * (1.0 / total)).astype(jnp.bfloat16))
        attn = jnp.concatenate(parts, axis=1)
        placed = jnp.dot(perm[...], attn, preferred_element_type=jnp.float32)
        sendbuf[h] = placed.astype(jnp.bfloat16).reshape(N, CAP, WQ)
        recvbuf[h, me] = sendbuf[h, me]
        relay_in(h).start()
        for k in DIRECT:
            row_copy(h, k).start()

    pl.semaphore_wait(barrier, len(greet))

    kv_lag = 3
    last = kv_lag + REACH
    stages = [(kv_lag + s, lambda h, s=s: forward(s, h)) for s in reversed(range(REACH))]
    stages += [(2, lambda h: swap_two(0, h)), (1, lambda h: swap_one(0, h))]
    stages += [(0, lambda h: swap_core(0, h))]
    stages += [(last - 1, lambda h: swap_two(1, h)), (last - 2, lambda h: swap_one(1, h))]
    stages += [(last - 3, lambda h: swap_core(1, h)), (last + 1, pass_on), (last, attend)]

    @pl.loop(0, KVH + last + 1)
    def _(t):
        for lag, stage in stages:
            h = t - lag

            @pl.when((h >= 0) & (h < KVH))
            def _():
                stage(h)

        @pl.when(t == 1)
        def _():
            tables()

    @pl.loop(0, KVH)
    def _(h):
        for k in DIRECT:
            row_copy(h, k).wait_recv()
        relay_out(h).wait_recv()

    @pl.loop(0, N)
    def _(i):
        square = jnp.zeros((CAP, WQ), jnp.float32)
        for h in range(KVH):
            part = recvbuf[h, i].astype(jnp.float32)
            square = square + part * part
        mean = jnp.sum(square, axis=1, keepdims=True) * (1.0 / WIDTH)
        norm = lax.rsqrt(mean + 1e-06)
        rows = pl.ds(pl.multiple_of(i * CAP, CAP), CAP)
        for h in range(KVH):
            cols = slice(h * WQ, (h + 1) * WQ)
            part = recvbuf[h, i].astype(jnp.float32)
            out[rows, cols] = (part * norm * gain[:, cols]).astype(jnp.bfloat16)

    @pl.loop(0, KVH)
    def _(h):
        for k in DIRECT:
            row_copy(h, k).wait_send()
        relay_in(h).wait_send()
        relay_out(h).wait_send()
        for s in range(REACH):

            @pl.when((me >= s) & (me < N - 1))
            def _():
                kv_copy(s, h).wait_send()

        for kind in (0, 1):
            core_copy(kind, h).wait_send()
            for b in (0, 1):
                all_three(kinds[kind][5], one_ss, kind, h, b)
                all_three(kinds[kind][7], two_ss, kind, h, b)


def shards(queries, key_values, doc_lengths, pairing, swap_ids, dest, gain):
    listed = swap_ids[0, 0]
    vmem = pl.BlockSpec(memory_space=pltpu.VMEM)
    hbm = pl.BlockSpec(memory_space=pltpu.HBM)
    dma = pltpu.SemaphoreType.DMA

    def swap_buffers(width):
        shapes = [(KVH, 2), (KVH, 2), (KVH, 2), (KVH, 2, 3), (KVH, 2), (KVH, 2, 3)]
        return [pltpu.VMEM((*shape, BLK, width), jnp.bfloat16) for shape in shapes]

    return pl.pallas_call(
        fused,
        name="attend_and_route",
        out_shape=jax.ShapeDtypeStruct((N * CAP, WIDTH), jnp.bfloat16),
        in_specs=[hbm] * 7,
        out_specs=vmem,
        scratch_shapes=[
            pltpu.SMEM((2,), jnp.int32),
            pltpu.SMEM((1, 8), jnp.int32),
            pltpu.SMEM((32,), jnp.int32),
            pltpu.VMEM((T, WIDTH), jnp.bfloat16),
            pltpu.VMEM((T, KVH * 2 * D), jnp.bfloat16),
            pltpu.VMEM((1, T), jnp.int32),
            pltpu.VMEM((1, WIDTH), jnp.float32),
            dma((7,)),
            pltpu.VMEM((SLOTS, KVH, T, 2 * D), jnp.bfloat16),
            pltpu.VMEM((KVH, N, CAP, WQ), jnp.bfloat16),
            pltpu.VMEM((KVH, N, CAP, WQ), jnp.bfloat16),
            pltpu.VMEM((KVH, CAP, WQ), jnp.bfloat16),
            pltpu.VMEM((T, KEYS), jnp.float32),
            pltpu.VMEM((N * CAP, T), jnp.bfloat16),
            *swap_buffers(2 * D),
            *swap_buffers(WQ),
            *(dma((SLOTS, KVH)) for _ in range(2)),
            *(dma((KVH, N)) for _ in range(2)),
            dma((2, KVH)),
            dma((KVH,)),
            *(dma((2, KVH)) for _ in range(2)),
            *(dma((2, KVH, 2)) for _ in range(4)),
        ],
        compiler_params=pltpu.CompilerParams(
            collective_id=0, has_side_effects=True, vmem_limit_bytes=48 << 20
        ),
    )(
        listed, doc_lengths, pairing, queries, key_values,
        dest.reshape(1, T), gain.reshape(1, WIDTH),
    )


def solution(mesh):
    return jax.shard_map(
        shards,
        mesh=mesh,
        in_specs=(
            P(("outer", "inner"), None),
            P(("outer", "inner"), None),
            P("outer", None),
            P(),
            P("outer", "inner", None),
            P(("outer", "inner"), None),
            P(),
        ),
        out_specs=P(("outer", "inner"), None),
        check_vma=False,
    )
```

```python
import math

import jax
import jax.numpy as jnp
from jax import lax
from jax.experimental import pallas as pl
from jax.experimental.pallas import tpu as pltpu
from jax.sharding import PartitionSpec as P

HEADS = 40
KVH = 8
D = 128
BLK = 32
PER = HEADS // KVH
WQ = PER * D
T = 128
N = 8
REACH = 4
SLOTS = REACH + 1
CAP = 32
HALF = T // 2
KEYS = SLOTS * T
NEG = -1e30
RELAYED = 6
DIRECT = (3, 5, 2, 6, 1, 7)
WIDTH = HEADS * D
MESH = pl.DeviceIdType.MESH


def fused(
    ids_hbm, lens_hbm, pair_hbm, q_hbm, kv_hbm, drow_hbm, gain_hbm, out,
    ids, lens, pair, q, kv, drow, gain, load_s,
    kvbuf, posbuf, sendbuf, recvbuf, relay, bias, perm,
    kv_own, kv_core, kv_mid, kv_in1, kv_far, kv_in2,
    q_own, q_core, q_mid, q_in1, q_far, q_in2,
    kv_ss, kv_rs, pos_ss, pos_rs, a_ss, a_rs, r_ss, r_rs, core_ss, core_rs, one_ss, one_rs, two_ss, two_rs,
):
    me = lax.axis_index("inner")
    seq = lax.axis_index("outer")
    core, y, x = lax.rem(seq, 2), lax.rem(seq // 2, 4), seq // 8

    def flipped(i, k):
        if k == 1:
            return i + 1 - 2 * lax.rem(i, 2)
        return i + 2 - 4 * (i // 2) if k == 2 else 3 - i

    other_core = seq + 1 - 2 * core
    peers = {
        "y": [seq + 2 * (flipped(y, k) - y) for k in (1, 2, 3)],
        "x": [seq + 8 * (flipped(x, k) - x) for k in (1, 2, 3)],
    }

    sources = (ids_hbm, pair_hbm, kv_hbm, q_hbm, drow_hbm, lens_hbm, gain_hbm)
    targets = (ids, pair, kv, q, drow, lens, gain)
    loads = [
        pltpu.make_async_copy(a, b, load_s.at[i]) for i, (a, b) in enumerate(zip(sources, targets))
    ]
    for load in loads:
        load.start()

    barrier = pltpu.get_barrier_semaphore()
    greet = [{"inner": lax.rem(me + k, N)} for k in range(1, N)]
    greet += [{"outer": g} for g in (other_core, *peers["y"], *peers["x"])]
    for device in greet:
        pl.semaphore_signal(barrier, inc=1, device_id=device, device_id_type=MESH)

    for load in loads:
        load.wait()
    id0, id1 = ids[0], ids[1]
    kept0 = jnp.where(id0 > 0, 0, jnp.where(id1 > 1, 1, 2))
    kept1 = jnp.where(id1 < 3, 3, jnp.where(id0 < 2, 2, 1))
    mask = pair[0]
    bits = {"core": lax.rem(mask, 2), "y": lax.rem(lax.div(mask, 2), 4), "x": lax.div(mask, 8)}

    def chosen(block, own, first, second):
        return jnp.where(id0 == block, first, jnp.where(id1 == block, second, own))

    def one_block(ref, cols, listed):
        value = ref[0:BLK, cols]
        for block in range(1, T // BLK):
            value = jnp.where(listed == block, ref[block * BLK : (block + 1) * BLK, cols], value)
        return value

    kinds = (
        (kv, 2 * D, kv_own, kv_core, kv_mid, kv_in1, kv_far, kv_in2),
        (q, WQ, q_own, q_core, q_mid, q_in1, q_far, q_in2),
    )
    routes = (("y", "x"), ("x", "y"))

    def core_copy(kind, h):
        _, _, mine, theirs, *_ = kinds[kind]
        return pltpu.make_async_remote_copy(
            src_ref=mine.at[h],
            dst_ref=theirs.at[h],
            send_sem=core_ss.at[kind, h],
            recv_sem=core_rs.at[kind, h],
            device_id={"outer": other_core},
            device_id_type=MESH,
        )

    def axis_copies(source, target, ss, rs, kind, h, b, axis):
        return [
            pltpu.make_async_remote_copy(
                src_ref=source.at[h, b],
                dst_ref=target.at[h, b, k],
                send_sem=ss.at[kind, h, b],
                recv_sem=rs.at[kind, h, b],
                device_id={"outer": peer},
                device_id_type=MESH,
            )
            for k, peer in enumerate(peers[axis])
        ]

    def all_three(target, sems, kind, h, b):
        whole = target.at[h, b]
        pltpu.make_async_copy(whole, whole, sems.at[kind, h, b]).wait()

    def picked(source, target, h, b, axis):
        v = bits[axis]
        value = source[h, b]
        for k in (1, 2, 3):
            value = jnp.where(v == k, target[h, b, k - 1], value)
        return value

    def swap_core(kind, h):
        ref, width, mine, *_ = kinds[kind]
        cols = pl.ds(pl.multiple_of(h * width, D), width)
        for b, listed in enumerate((id0, id1)):
            mine[h, b] = one_block(ref, cols, listed)
        core_copy(kind, h).start()

    def swap_one(kind, h):
        _, _, mine, theirs, mid, in1, _, _ = kinds[kind]
        core_copy(kind, h).wait_recv()
        mid[h] = jnp.where(bits["core"] == 1, theirs[h], mine[h])
        for b in (0, 1):
            for copy in axis_copies(mid, in1, one_ss, one_rs, kind, h, b, routes[b][0]):
                copy.start()

    def swap_two(kind, h):
        _, _, _, _, mid, in1, far, in2 = kinds[kind]
        for b in (0, 1):
            all_three(in1, one_rs, kind, h, b)
            far[h, b] = picked(mid, in1, h, b, routes[b][0])
            for copy in axis_copies(far, in2, two_ss, two_rs, kind, h, b, routes[b][1]):
                copy.start()

    def swapped(kind, h):
        _, _, _, _, _, _, far, in2 = kinds[kind]
        for b in (0, 1):
            all_three(in2, two_rs, kind, h, b)
        return [picked(far, in2, h, b, routes[b][1]) for b in (0, 1)]

    def tables():
        for s in range(1, SLOTS):

            @pl.when(me < s)
            def _():
                kvbuf[s] = jnp.zeros(kvbuf.shape[1:], kvbuf.dtype)
                posbuf[s] = jnp.full(posbuf.shape[1:], -1, jnp.int32)

        qpos = me * T + lax.broadcasted_iota(jnp.int32, (T, T), 0)
        start = jnp.zeros((T, T), jnp.int32)
        end = lens[0, 0]
        for k in range(1, 9):
            start = jnp.where(qpos >= end, jnp.maximum(start, end), start)
            if k < 8:
                end = end + lens[0, k]
        for s in range(SLOTS):
            if s > 0:

                @pl.when(me >= s)
                def _():
                    pos_copy(s).wait_recv()

            kpos = posbuf[s, 0:1, :]
            bias[:, s * T : (s + 1) * T] = jnp.where((kpos <= qpos) & (kpos >= start), 0.0, NEG)

        first = lax.broadcasted_iota(jnp.int32, (T, T), 0)
        second = lax.broadcasted_iota(jnp.int32, (T, T), 1)
        row = drow[...].astype(jnp.float32)
        column = jnp.sum(jnp.where(first == second, row, 0.0), axis=1, keepdims=True)
        same = (column == row) & (first < second)
        rank = jnp.sum(same.astype(jnp.int32), axis=0, keepdims=True)
        place = drow[...] * CAP + rank
        slot = lax.broadcasted_iota(jnp.int32, (N * CAP, T), 0)
        perm[...] = (slot == place).astype(jnp.float32).astype(jnp.bfloat16)

    def kv_copy(s, h, half):
        rows = slice(half * HALF, (half + 1) * HALF)
        return pltpu.make_async_remote_copy(
            src_ref=kvbuf.at[s, h, rows],
            dst_ref=kvbuf.at[s + 1, h, rows],
            send_sem=kv_ss.at[half, s, h],
            recv_sem=kv_rs.at[half, s + 1, h],
            device_id={"inner": lax.rem(me + 1, N)},
            device_id_type=MESH,
        )

    def pos_copy(s):
        return pltpu.make_async_remote_copy(
            src_ref=posbuf.at[0],
            dst_ref=posbuf.at[s],
            send_sem=pos_ss.at[s],
            recv_sem=pos_rs.at[s],
            device_id={"inner": lax.rem(me + s, N)},
            device_id_type=MESH,
        )

    def positions():
        lane = lax.broadcasted_iota(jnp.int32, posbuf.shape[1:], 1)
        part = lane // BLK
        block = jnp.where(
            part == 0, kept0, jnp.where(part == 1, kept1, jnp.where(part == 2, id0, id1))
        )
        posbuf[0] = me * T + block * BLK + lax.rem(lane, BLK)
        for s in range(1, SLOTS):

            @pl.when(me < N - s)
            def _():
                pos_copy(s).start()

    def row_copy(h, k):
        to = lax.rem(me + k, N)
        return pltpu.make_async_remote_copy(
            src_ref=sendbuf.at[h, to],
            dst_ref=recvbuf.at[h, me],
            send_sem=a_ss.at[h, k],
            recv_sem=a_rs.at[h, k],
            device_id={"inner": to},
            device_id_type=MESH,
        )

    def relay_in(h):
        return pltpu.make_async_remote_copy(
            src_ref=sendbuf.at[h, lax.rem(me + 4, N)],
            dst_ref=relay.at[h],
            send_sem=r_ss.at[0, h],
            recv_sem=r_rs.at[h],
            device_id={"inner": lax.rem(me + 6, N)},
            device_id_type=MESH,
        )

    def relay_out(h):
        return pltpu.make_async_remote_copy(
            src_ref=relay.at[h],
            dst_ref=recvbuf.at[h, lax.rem(me + 2, N)],
            send_sem=r_ss.at[1, h],
            recv_sem=a_rs.at[h, 4],
            device_id={"inner": lax.rem(me + 6, N)},
            device_id_type=MESH,
        )

    def pass_on(h):
        @pl.when(h < RELAYED)
        def _():
            relay_in(h).wait_recv()
            relay_out(h).start()

    def forward(s, h, half):
        if s > 0:

            @pl.when(me >= s)
            def _():
                kv_copy(s - 1, h, half).wait_recv()

        elif half == 0:
            cols = pl.ds(pl.multiple_of(h * 2 * D, D), 2 * D)
            kvbuf[0, h, :BLK, :] = one_block(kv, cols, kept0)
            kvbuf[0, h, BLK:HALF, :] = one_block(kv, cols, kept1)
        else:
            r0, r1 = swapped(0, h)
            kvbuf[0, h, HALF : HALF + BLK, :] = r0
            kvbuf[0, h, HALF + BLK :, :] = r1

        @pl.when((me >= s) & (me < N - 1))
        def _():
            kv_copy(s, h, half).start()

    factor = math.log2(math.e) / math.sqrt(D)

    def attend(h):
        @pl.when(me >= REACH)
        def _():
            for half in (0, 1):
                kv_copy(REACH - 1, h, half).wait_recv()

        own = q[:, pl.ds(pl.multiple_of(h * WQ, D), WQ)]
        r0, r1 = swapped(1, h)
        qh = jnp.concatenate(
            [chosen(b, own[b * BLK : (b + 1) * BLK], r0, r1) for b in range(T // BLK)], axis=0
        )
        keys = kvbuf[:, h, :, :D].reshape(KEYS, D)
        values = kvbuf[:, h, :, D:].reshape(KEYS, D)
        parts = []
        for g in range(PER):
            s = lax.dot_general(
                qh[:, g * D : (g + 1) * D],
                keys,
                (((1,), (1,)), ((), ())),
                preferred_element_type=jnp.float32,
            )
            s = s + bias[...]
            expo = jnp.exp2((s - jnp.max(s, axis=1, keepdims=True)) * factor)
            total = jnp.sum(expo, axis=1, keepdims=True)
            acc = jnp.dot(expo.astype(jnp.bfloat16), values, preferred_element_type=jnp.float32)
            parts.append((acc * (1.0 / total)).astype(jnp.bfloat16))
        attn = jnp.concatenate(parts, axis=1)
        placed = jnp.dot(perm[...], attn, preferred_element_type=jnp.float32)
        sendbuf[h] = placed.astype(jnp.bfloat16).reshape(N, CAP, WQ)
        recvbuf[h, me] = sendbuf[h, me]
        @pl.when(h < RELAYED)
        def _():
            relay_in(h).start()

        @pl.when(h >= RELAYED)
        def _():
            row_copy(h, 4).start()

        for k in DIRECT:
            row_copy(h, k).start()

    pl.semaphore_wait(barrier, len(greet))

    kv_lag = 3
    last = kv_lag + REACH
    stages = [(kv_lag + s, lambda h, s=s: forward(s, h, 1)) for s in reversed(range(REACH))]
    stages += [(2, lambda h: swap_two(0, h)), (1, lambda h: swap_one(0, h))]
    stages += [(0, lambda h: swap_core(0, h))]
    stages += [(s, lambda h, s=s: forward(s, h, 0)) for s in reversed(range(REACH))]
    stages += [(last - 1, lambda h: swap_two(1, h)), (last - 2, lambda h: swap_one(1, h))]
    stages += [(last - 3, lambda h: swap_core(1, h)), (last + 1, pass_on), (last, attend)]

    @pl.loop(0, KVH + last + 1)
    def _(t):
        for lag, stage in stages:
            h = t - lag

            @pl.when((h >= 0) & (h < KVH))
            def _():
                stage(h)

        @pl.when(t == 0)
        def _():
            positions()

        @pl.when(t == 3)
        def _():
            tables()

    @pl.loop(0, KVH)
    def _(h):
        for k in DIRECT:
            row_copy(h, k).wait_recv()
        relay_out(h).wait_recv()

    @pl.loop(0, N)
    def _(i):
        square = jnp.zeros((CAP, WQ), jnp.float32)
        for h in range(KVH):
            part = recvbuf[h, i].astype(jnp.float32)
            square = square + part * part
        mean = jnp.sum(square, axis=1, keepdims=True) * (1.0 / WIDTH)
        norm = lax.rsqrt(mean + 1e-06)
        rows = pl.ds(pl.multiple_of(i * CAP, CAP), CAP)
        for h in range(KVH):
            cols = slice(h * WQ, (h + 1) * WQ)
            part = recvbuf[h, i].astype(jnp.float32)
            out[rows, cols] = (part * norm * gain[:, cols]).astype(jnp.bfloat16)

    for s in range(1, SLOTS):

        @pl.when(me < N - s)
        def _():
            pos_copy(s).wait_send()

    @pl.loop(0, KVH)
    def _(h):
        for k in DIRECT:
            row_copy(h, k).wait_send()
        @pl.when(h < RELAYED)
        def _():
            relay_in(h).wait_send()
            relay_out(h).wait_send()

        @pl.when(h >= RELAYED)
        def _():
            row_copy(h, 4).wait_send()
        for s in range(REACH):

            @pl.when((me >= s) & (me < N - 1))
            def _():
                for half in (0, 1):
                    kv_copy(s, h, half).wait_send()

        for kind in (0, 1):
            core_copy(kind, h).wait_send()
            for b in (0, 1):
                all_three(kinds[kind][5], one_ss, kind, h, b)
                all_three(kinds[kind][7], two_ss, kind, h, b)


def shards(queries, key_values, doc_lengths, pairing, swap_ids, dest, gain):
    listed = swap_ids[0, 0]
    vmem = pl.BlockSpec(memory_space=pltpu.VMEM)
    hbm = pl.BlockSpec(memory_space=pltpu.HBM)
    dma = pltpu.SemaphoreType.DMA

    def swap_buffers(width):
        shapes = [(KVH, 2), (KVH, 2), (KVH, 2), (KVH, 2, 3), (KVH, 2), (KVH, 2, 3)]
        return [pltpu.VMEM((*shape, BLK, width), jnp.bfloat16) for shape in shapes]

    return pl.pallas_call(
        fused,
        name="attend_and_route",
        out_shape=jax.ShapeDtypeStruct((N * CAP, WIDTH), jnp.bfloat16),
        in_specs=[hbm] * 7,
        out_specs=vmem,
        scratch_shapes=[
            pltpu.SMEM((2,), jnp.int32),
            pltpu.SMEM((1, 8), jnp.int32),
            pltpu.SMEM((32,), jnp.int32),
            pltpu.VMEM((T, WIDTH), jnp.bfloat16),
            pltpu.VMEM((T, KVH * 2 * D), jnp.bfloat16),
            pltpu.VMEM((1, T), jnp.int32),
            pltpu.VMEM((1, WIDTH), jnp.float32),
            dma((7,)),
            pltpu.VMEM((SLOTS, KVH, T, 2 * D), jnp.bfloat16),
            pltpu.VMEM((SLOTS, 8, T), jnp.int32),
            pltpu.VMEM((KVH, N, CAP, WQ), jnp.bfloat16),
            pltpu.VMEM((KVH, N, CAP, WQ), jnp.bfloat16),
            pltpu.VMEM((KVH, CAP, WQ), jnp.bfloat16),
            pltpu.VMEM((T, KEYS), jnp.float32),
            pltpu.VMEM((N * CAP, T), jnp.bfloat16),
            *swap_buffers(2 * D),
            *swap_buffers(WQ),
            *(dma((2, SLOTS, KVH)) for _ in range(2)),
            *(dma((SLOTS,)) for _ in range(2)),
            *(dma((KVH, N)) for _ in range(2)),
            dma((2, KVH)),
            dma((KVH,)),
            *(dma((2, KVH)) for _ in range(2)),
            *(dma((2, KVH, 2)) for _ in range(4)),
        ],
        compiler_params=pltpu.CompilerParams(
            collective_id=0, has_side_effects=True, vmem_limit_bytes=60 << 20
        ),
    )(
        listed, doc_lengths, pairing, queries, key_values,
        dest.reshape(1, T), gain.reshape(1, WIDTH),
    )


def solution(mesh):
    return jax.shard_map(
        shards,
        mesh=mesh,
        in_specs=(
            P(("outer", "inner"), None),
            P(("outer", "inner"), None),
            P("outer", None),
            P(),
            P("outer", "inner", None),
            P(("outer", "inner"), None),
            P(),
        ),
        out_specs=P(("outer", "inner"), None),
        check_vma=False,
    )
```

```python
import math

import jax
import jax.numpy as jnp
from jax import lax
from jax.experimental import pallas as pl
from jax.experimental.pallas import tpu as pltpu
from jax.sharding import PartitionSpec as P

HEADS = 40
KVH = 8
D = 128
BLK = 32
PER = HEADS // KVH
WQ = PER * D
T = 128
N = 8
REACH = 4
SLOTS = REACH + 1
CAP = 32
HALF = T // 2
KEYS = SLOTS * T
NEG = -1e30
RELAYED = 6
DIRECT = (3, 5, 2, 6, 1, 7)
WIDTH = HEADS * D
MESH = pl.DeviceIdType.MESH


def fused(
    ids_hbm, lens_hbm, pair_hbm, q_hbm, kv_hbm, drow_hbm, gain_hbm, out,
    ids, lens, pair, q, kv, drow, gain, load_s,
    kvbuf, posbuf, sendbuf, recvbuf, relay, bias, perm,
    kv_own, kv_core, kv_mid, kv_in1, kv_far, kv_in2,
    q_own, q_core, q_mid, q_in1, q_far, q_in2,
    kv_ss, kv_rs, pos_ss, pos_rs, a_ss, a_rs, r_ss, r_rs, core_ss, core_rs, one_ss, one_rs, two_ss, two_rs,
):
    me = lax.axis_index("inner")
    seq = lax.axis_index("outer")
    core, y, x = lax.rem(seq, 2), lax.rem(seq // 2, 4), seq // 8

    def flipped(i, k):
        if k == 1:
            return i + 1 - 2 * lax.rem(i, 2)
        return i + 2 - 4 * (i // 2) if k == 2 else 3 - i

    other_core = seq + 1 - 2 * core
    peers = {
        "y": [seq + 2 * (flipped(y, k) - y) for k in (1, 2, 3)],
        "x": [seq + 8 * (flipped(x, k) - x) for k in (1, 2, 3)],
    }

    sources = (ids_hbm, pair_hbm, kv_hbm, q_hbm, drow_hbm, lens_hbm, gain_hbm)
    targets = (ids, pair, kv, q, drow, lens, gain)
    loads = [
        pltpu.make_async_copy(a, b, load_s.at[i]) for i, (a, b) in enumerate(zip(sources, targets))
    ]
    for load in loads:
        load.start()

    barrier = pltpu.get_barrier_semaphore()
    greet = [{"inner": lax.rem(me + k, N)} for k in range(1, N)]
    greet += [{"outer": g} for g in (other_core, *peers["y"], *peers["x"])]
    for device in greet:
        pl.semaphore_signal(barrier, inc=1, device_id=device, device_id_type=MESH)

    for load in loads:
        load.wait()
    id0, id1 = ids[0], ids[1]
    kept0 = jnp.where(id0 > 0, 0, jnp.where(id1 > 1, 1, 2))
    kept1 = jnp.where(id1 < 3, 3, jnp.where(id0 < 2, 2, 1))
    mask = pair[0]
    bits = {"core": lax.rem(mask, 2), "y": lax.rem(lax.div(mask, 2), 4), "x": lax.div(mask, 8)}

    def chosen(block, own, first, second):
        return jnp.where(id0 == block, first, jnp.where(id1 == block, second, own))

    def one_block(ref, cols, listed):
        value = ref[0:BLK, cols]
        for block in range(1, T // BLK):
            value = jnp.where(listed == block, ref[block * BLK : (block + 1) * BLK, cols], value)
        return value

    kinds = (
        (kv, 2 * D, kv_own, kv_core, kv_mid, kv_in1, kv_far, kv_in2),
        (q, WQ, q_own, q_core, q_mid, q_in1, q_far, q_in2),
    )
    routes = (("y", "x"), ("x", "y"))

    def core_copy(kind, h):
        _, _, mine, theirs, *_ = kinds[kind]
        return pltpu.make_async_remote_copy(
            src_ref=mine.at[h],
            dst_ref=theirs.at[h],
            send_sem=core_ss.at[kind, h],
            recv_sem=core_rs.at[kind, h],
            device_id={"outer": other_core},
            device_id_type=MESH,
        )

    def axis_copies(source, target, ss, rs, kind, h, b, axis):
        return [
            pltpu.make_async_remote_copy(
                src_ref=source.at[h, b],
                dst_ref=target.at[h, b, k],
                send_sem=ss.at[kind, h, b],
                recv_sem=rs.at[kind, h, b],
                device_id={"outer": peer},
                device_id_type=MESH,
            )
            for k, peer in enumerate(peers[axis])
        ]

    def all_three(target, sems, kind, h, b):
        whole = target.at[h, b]
        pltpu.make_async_copy(whole, whole, sems.at[kind, h, b]).wait()

    def picked(source, target, h, b, axis):
        v = bits[axis]
        value = source[h, b]
        for k in (1, 2, 3):
            value = jnp.where(v == k, target[h, b, k - 1], value)
        return value

    def swap_core(kind, h):
        ref, width, mine, *_ = kinds[kind]
        cols = pl.ds(pl.multiple_of(h * width, D), width)
        for b, listed in enumerate((id0, id1)):
            mine[h, b] = one_block(ref, cols, listed)
        core_copy(kind, h).start()

    def swap_one(kind, h):
        _, _, mine, theirs, mid, in1, _, _ = kinds[kind]
        core_copy(kind, h).wait_recv()
        mid[h] = jnp.where(bits["core"] == 1, theirs[h], mine[h])
        for b in (0, 1):
            for copy in axis_copies(mid, in1, one_ss, one_rs, kind, h, b, routes[b][0]):
                copy.start()

    def swap_two(kind, h):
        _, _, _, _, mid, in1, far, in2 = kinds[kind]
        for b in (0, 1):
            all_three(in1, one_rs, kind, h, b)
            far[h, b] = picked(mid, in1, h, b, routes[b][0])
            for copy in axis_copies(far, in2, two_ss, two_rs, kind, h, b, routes[b][1]):
                copy.start()

    def swapped(kind, h):
        _, _, _, _, _, _, far, in2 = kinds[kind]
        for b in (0, 1):
            all_three(in2, two_rs, kind, h, b)
        return [picked(far, in2, h, b, routes[b][1]) for b in (0, 1)]

    def tables():
        for s in range(1, SLOTS):

            @pl.when(me < s)
            def _():
                kvbuf[s] = jnp.zeros(kvbuf.shape[1:], kvbuf.dtype)
                posbuf[s] = jnp.full(posbuf.shape[1:], -1, jnp.int32)

        qpos = me * T + lax.broadcasted_iota(jnp.int32, (T, T), 0)
        start = jnp.zeros((T, T), jnp.int32)
        end = lens[0, 0]
        for k in range(1, 9):
            start = jnp.where(qpos >= end, jnp.maximum(start, end), start)
            if k < 8:
                end = end + lens[0, k]
        for s in range(SLOTS):
            if s > 0:

                @pl.when(me >= s)
                def _():
                    pos_copy(s).wait_recv()

            kpos = posbuf[s, 0:1, :]
            bias[:, s * T : (s + 1) * T] = jnp.where((kpos <= qpos) & (kpos >= start), 0.0, NEG)

        first = lax.broadcasted_iota(jnp.int32, (T, T), 0)
        second = lax.broadcasted_iota(jnp.int32, (T, T), 1)
        row = drow[...].astype(jnp.float32)
        column = jnp.sum(jnp.where(first == second, row, 0.0), axis=1, keepdims=True)
        same = (column == row) & (first < second)
        rank = jnp.sum(same.astype(jnp.int32), axis=0, keepdims=True)
        place = drow[...] * CAP + rank
        slot = lax.broadcasted_iota(jnp.int32, (N * CAP, T), 0)
        perm[...] = (slot == place).astype(jnp.float32).astype(jnp.bfloat16)

    def kv_copy(s, h, half):
        rows = slice(half * HALF, (half + 1) * HALF)
        return pltpu.make_async_remote_copy(
            src_ref=kvbuf.at[s, h, rows],
            dst_ref=kvbuf.at[s + 1, h, rows],
            send_sem=kv_ss.at[half, s, h],
            recv_sem=kv_rs.at[half, s + 1, h],
            device_id={"inner": lax.rem(me + 1, N)},
            device_id_type=MESH,
        )

    def pos_copy(s):
        return pltpu.make_async_remote_copy(
            src_ref=posbuf.at[0],
            dst_ref=posbuf.at[s],
            send_sem=pos_ss.at[s],
            recv_sem=pos_rs.at[s],
            device_id={"inner": lax.rem(me + s, N)},
            device_id_type=MESH,
        )

    def positions():
        lane = lax.broadcasted_iota(jnp.int32, posbuf.shape[1:], 1)
        part = lane // BLK
        block = jnp.where(
            part == 0, kept0, jnp.where(part == 1, kept1, jnp.where(part == 2, id0, id1))
        )
        posbuf[0] = me * T + block * BLK + lax.rem(lane, BLK)
        for s in range(1, SLOTS):

            @pl.when(me < N - s)
            def _():
                pos_copy(s).start()

    def row_copy(h, k):
        to = lax.rem(me + k, N)
        return pltpu.make_async_remote_copy(
            src_ref=sendbuf.at[h, to],
            dst_ref=recvbuf.at[h, me],
            send_sem=a_ss.at[h, k],
            recv_sem=a_rs.at[h, k],
            device_id={"inner": to},
            device_id_type=MESH,
        )

    def relay_in(h):
        return pltpu.make_async_remote_copy(
            src_ref=sendbuf.at[h, lax.rem(me + 4, N)],
            dst_ref=relay.at[h],
            send_sem=r_ss.at[0, h],
            recv_sem=r_rs.at[h],
            device_id={"inner": lax.rem(me + 6, N)},
            device_id_type=MESH,
        )

    def relay_out(h):
        return pltpu.make_async_remote_copy(
            src_ref=relay.at[h],
            dst_ref=recvbuf.at[h, lax.rem(me + 2, N)],
            send_sem=r_ss.at[1, h],
            recv_sem=a_rs.at[h, 4],
            device_id={"inner": lax.rem(me + 6, N)},
            device_id_type=MESH,
        )

    def pass_on(h):
        @pl.when(h < RELAYED)
        def _():
            relay_in(h).wait_recv()
            relay_out(h).start()

    def forward(s, h, half):
        if s > 0:

            @pl.when(me >= s)
            def _():
                kv_copy(s - 1, h, half).wait_recv()

        elif half == 0:
            cols = pl.ds(pl.multiple_of(h * 2 * D, D), 2 * D)
            kvbuf[0, h, :BLK, :] = one_block(kv, cols, kept0)
            kvbuf[0, h, BLK:HALF, :] = one_block(kv, cols, kept1)
        else:
            r0, r1 = swapped(0, h)
            kvbuf[0, h, HALF : HALF + BLK, :] = r0
            kvbuf[0, h, HALF + BLK :, :] = r1

        @pl.when((me >= s) & (me < N - 1))
        def _():
            kv_copy(s, h, half).start()

    factor = math.log2(math.e) / math.sqrt(D)

    def attend(h):
        @pl.when(me >= REACH)
        def _():
            for half in (0, 1):
                kv_copy(REACH - 1, h, half).wait_recv()

        own = q[:, pl.ds(pl.multiple_of(h * WQ, D), WQ)]
        r0, r1 = swapped(1, h)
        qh = jnp.concatenate(
            [chosen(b, own[b * BLK : (b + 1) * BLK], r0, r1) for b in range(T // BLK)], axis=0
        )
        keys = kvbuf[:, h, :, :D].reshape(KEYS, D)
        values = kvbuf[:, h, :, D:].reshape(KEYS, D)
        parts = []
        for g in range(PER):
            s = lax.dot_general(
                qh[:, g * D : (g + 1) * D],
                keys,
                (((1,), (1,)), ((), ())),
                preferred_element_type=jnp.float32,
            )
            s = s + bias[...]
            expo = jnp.exp2((s - jnp.max(s, axis=1, keepdims=True)) * factor)
            total = jnp.sum(expo, axis=1, keepdims=True)
            acc = jnp.dot(expo.astype(jnp.bfloat16), values, preferred_element_type=jnp.float32)
            parts.append((acc * (1.0 / total)).astype(jnp.bfloat16))
        attn = jnp.concatenate(parts, axis=1)
        placed = jnp.dot(perm[...], attn, preferred_element_type=jnp.float32)
        sendbuf[h] = placed.astype(jnp.bfloat16).reshape(N, CAP, WQ)
        recvbuf[h, me] = sendbuf[h, me]
        @pl.when(h < RELAYED)
        def _():
            relay_in(h).start()

        @pl.when(h >= RELAYED)
        def _():
            row_copy(h, 4).start()

        for k in DIRECT:
            row_copy(h, k).start()

    pl.semaphore_wait(barrier, len(greet))

    kv_lag = 3
    last = kv_lag + REACH
    stages = [(kv_lag + s, lambda h, s=s: forward(s, h, 1)) for s in reversed(range(REACH))]
    stages += [(2, lambda h: swap_two(0, h)), (1, lambda h: swap_one(0, h))]
    stages += [(0, lambda h: swap_core(0, h))]
    stages += [(s, lambda h, s=s: forward(s, h, 0)) for s in reversed(range(REACH))]
    stages += [(last - 1, lambda h: swap_two(1, h)), (last - 2, lambda h: swap_one(1, h))]
    stages += [(last - 3, lambda h: swap_core(1, h)), (last + 1, pass_on), (last, attend)]

    @pl.loop(0, KVH + last + 1)
    def _(t):
        for lag, stage in stages:
            h = t - lag

            @pl.when((h >= 0) & (h < KVH))
            def _():
                stage(h)

        @pl.when(t == 0)
        def _():
            positions()

        @pl.when(t == 3)
        def _():
            tables()

    @pl.loop(0, KVH)
    def _(h):
        for k in DIRECT:
            row_copy(h, k).wait_recv()
        relay_out(h).wait_recv()

    @pl.loop(0, N)
    def _(i):
        square = jnp.zeros((CAP, WQ), jnp.float32)
        for h in range(KVH):
            part = recvbuf[h, i].astype(jnp.float32)
            square = square + part * part
        mean = jnp.sum(square, axis=1, keepdims=True) * (1.0 / WIDTH)
        norm = lax.rsqrt(mean + 1e-06)
        rows = pl.ds(pl.multiple_of(i * CAP, CAP), CAP)
        for h in range(KVH):
            cols = slice(h * WQ, (h + 1) * WQ)
            part = recvbuf[h, i].astype(jnp.float32)
            out[rows, cols] = (part * norm * gain[:, cols]).astype(jnp.bfloat16)

    for s in range(1, SLOTS):

        @pl.when(me < N - s)
        def _():
            pos_copy(s).wait_send()

    @pl.loop(0, KVH)
    def _(h):
        for k in DIRECT:
            row_copy(h, k).wait_send()
        @pl.when(h < RELAYED)
        def _():
            relay_in(h).wait_send()
            relay_out(h).wait_send()

        @pl.when(h >= RELAYED)
        def _():
            row_copy(h, 4).wait_send()
        for s in range(REACH):

            @pl.when((me >= s) & (me < N - 1))
            def _():
                for half in (0, 1):
                    kv_copy(s, h, half).wait_send()

        for kind in (0, 1):
            core_copy(kind, h).wait_send()
            for b in (0, 1):
                all_three(kinds[kind][5], one_ss, kind, h, b)
                all_three(kinds[kind][7], two_ss, kind, h, b)


def shards(queries, key_values, doc_lengths, pairing, swap_ids, dest, gain):
    listed = swap_ids[0, 0]
    vmem = pl.BlockSpec(memory_space=pltpu.VMEM)
    hbm = pl.BlockSpec(memory_space=pltpu.HBM)
    dma = pltpu.SemaphoreType.DMA

    def swap_buffers(width):
        shapes = [(KVH, 2), (KVH, 2), (KVH, 2), (KVH, 2, 3), (KVH, 2), (KVH, 2, 3)]
        return [pltpu.VMEM((*shape, BLK, width), jnp.bfloat16) for shape in shapes]

    return pl.pallas_call(
        fused,
        name="attend_and_route",
        out_shape=jax.ShapeDtypeStruct((N * CAP, WIDTH), jnp.bfloat16),
        in_specs=[hbm] * 7,
        out_specs=vmem,
        scratch_shapes=[
            pltpu.SMEM((2,), jnp.int32),
            pltpu.SMEM((1, 8), jnp.int32),
            pltpu.SMEM((32,), jnp.int32),
            pltpu.VMEM((T, WIDTH), jnp.bfloat16),
            pltpu.VMEM((T, KVH * 2 * D), jnp.bfloat16),
            pltpu.VMEM((1, T), jnp.int32),
            pltpu.VMEM((1, WIDTH), jnp.float32),
            dma((7,)),
            pltpu.VMEM((SLOTS, KVH, T, 2 * D), jnp.bfloat16),
            pltpu.VMEM((SLOTS, 8, T), jnp.int32),
            pltpu.VMEM((KVH, N, CAP, WQ), jnp.bfloat16),
            pltpu.VMEM((KVH, N, CAP, WQ), jnp.bfloat16),
            pltpu.VMEM((KVH, CAP, WQ), jnp.bfloat16),
            pltpu.VMEM((T, KEYS), jnp.float32),
            pltpu.VMEM((N * CAP, T), jnp.bfloat16),
            *swap_buffers(2 * D),
            *swap_buffers(WQ),
            *(dma((2, SLOTS, KVH)) for _ in range(2)),
            *(dma((SLOTS,)) for _ in range(2)),
            *(dma((KVH, N)) for _ in range(2)),
            dma((2, KVH)),
            dma((KVH,)),
            *(dma((2, KVH)) for _ in range(2)),
            *(dma((2, KVH, 2)) for _ in range(4)),
        ],
        compiler_params=pltpu.CompilerParams(
            collective_id=0, has_side_effects=True, vmem_limit_bytes=48 << 20
        ),
    )(
        *(
            pltpu.with_memory_space_constraint(a, pltpu.HBM)
            for a in (
                listed, doc_lengths, pairing, queries, key_values,
                dest.reshape(1, T), gain.reshape(1, WIDTH),
            )
        )
    )


def solution(mesh):
    return jax.shard_map(
        shards,
        mesh=mesh,
        in_specs=(
            P(("outer", "inner"), None),
            P(("outer", "inner"), None),
            P("outer", None),
            P(),
            P("outer", "inner", None),
            P(("outer", "inner"), None),
            P(),
        ),
        out_specs=P(("outer", "inner"), None),
        check_vma=False,
    )
```

```python
import math

import jax
import jax.numpy as jnp
from jax import lax
from jax.experimental import pallas as pl
from jax.experimental.pallas import tpu as pltpu
from jax.sharding import PartitionSpec as P

HEADS = 40
KVH = 8
D = 128
BLK = 32
PER = HEADS // KVH
WQ = PER * D
T = 128
N = 8
REACH = 4
SLOTS = REACH + 1
CAP = 32
HALF = T // 2
KEYS = SLOTS * T
NEG = -1e30
RELAYED = 6
DIRECT = (3, 5, 2, 6, 1, 7)
WIDTH = HEADS * D
MESH = pl.DeviceIdType.MESH


def fused(
    ids_hbm, lens_hbm, pair_hbm, q_hbm, kv_hbm, drow_hbm, gain_hbm, out,
    ids, lens, pair, q, kv, drow, gain, load_s,
    kvbuf, posbuf, sendbuf, recvbuf, relay, squares, bias, perm,
    kv_own, kv_core, kv_mid, kv_in1, kv_far, kv_in2,
    q_own, q_core, q_mid, q_in1, q_far, q_in2,
    kv_ss, kv_rs, pos_ss, pos_rs, a_ss, a_rs, r_ss, r_rs, core_ss, core_rs, one_ss, one_rs, two_ss, two_rs,
):
    me = lax.axis_index("inner")
    seq = lax.axis_index("outer")
    core, y, x = lax.rem(seq, 2), lax.rem(seq // 2, 4), seq // 8

    def flipped(i, k):
        if k == 1:
            return i + 1 - 2 * lax.rem(i, 2)
        return i + 2 - 4 * (i // 2) if k == 2 else 3 - i

    other_core = seq + 1 - 2 * core
    peers = {
        "y": [seq + 2 * (flipped(y, k) - y) for k in (1, 2, 3)],
        "x": [seq + 8 * (flipped(x, k) - x) for k in (1, 2, 3)],
    }

    sources = (ids_hbm, pair_hbm, kv_hbm, q_hbm, drow_hbm, lens_hbm, gain_hbm)
    targets = (ids, pair, kv, q, drow, lens, gain)
    loads = [
        pltpu.make_async_copy(a, b, load_s.at[i]) for i, (a, b) in enumerate(zip(sources, targets))
    ]
    for load in loads:
        load.start()

    barrier = pltpu.get_barrier_semaphore()
    greet = [{"inner": lax.rem(me + k, N)} for k in range(1, N)]
    greet += [{"outer": g} for g in (other_core, *peers["y"], *peers["x"])]
    for device in greet:
        pl.semaphore_signal(barrier, inc=1, device_id=device, device_id_type=MESH)

    for load in loads[:3]:
        load.wait()
    id0, id1 = ids[0], ids[1]
    kept0 = jnp.where(id0 > 0, 0, jnp.where(id1 > 1, 1, 2))
    kept1 = jnp.where(id1 < 3, 3, jnp.where(id0 < 2, 2, 1))
    mask = pair[0]
    bits = {"core": lax.rem(mask, 2), "y": lax.rem(lax.div(mask, 2), 4), "x": lax.div(mask, 8)}

    def chosen(block, own, first, second):
        return jnp.where(id0 == block, first, jnp.where(id1 == block, second, own))

    def one_block(ref, cols, listed):
        value = ref[0:BLK, cols]
        for block in range(1, T // BLK):
            value = jnp.where(listed == block, ref[block * BLK : (block + 1) * BLK, cols], value)
        return value

    kinds = (
        (kv, 2 * D, kv_own, kv_core, kv_mid, kv_in1, kv_far, kv_in2),
        (q, WQ, q_own, q_core, q_mid, q_in1, q_far, q_in2),
    )
    routes = (("y", "x"), ("x", "y"))

    def core_copy(kind, h):
        _, _, mine, theirs, *_ = kinds[kind]
        return pltpu.make_async_remote_copy(
            src_ref=mine.at[h],
            dst_ref=theirs.at[h],
            send_sem=core_ss.at[kind, h],
            recv_sem=core_rs.at[kind, h],
            device_id={"outer": other_core},
            device_id_type=MESH,
        )

    def axis_copies(source, target, ss, rs, kind, h, b, axis):
        return [
            pltpu.make_async_remote_copy(
                src_ref=source.at[h, b],
                dst_ref=target.at[h, b, k],
                send_sem=ss.at[kind, h, b],
                recv_sem=rs.at[kind, h, b],
                device_id={"outer": peer},
                device_id_type=MESH,
            )
            for k, peer in enumerate(peers[axis])
        ]

    def all_three(target, sems, kind, h, b):
        whole = target.at[h, b]
        pltpu.make_async_copy(whole, whole, sems.at[kind, h, b]).wait()

    def picked(source, target, h, b, axis):
        v = bits[axis]
        value = source[h, b]
        for k in (1, 2, 3):
            value = jnp.where(v == k, target[h, b, k - 1], value)
        return value

    def swap_core(kind, h):
        ref, width, mine, *_ = kinds[kind]
        cols = pl.ds(pl.multiple_of(h * width, D), width)
        for b, listed in enumerate((id0, id1)):
            mine[h, b] = one_block(ref, cols, listed)
        core_copy(kind, h).start()

    def swap_one(kind, h):
        _, _, mine, theirs, mid, in1, _, _ = kinds[kind]
        core_copy(kind, h).wait_recv()
        mid[h] = jnp.where(bits["core"] == 1, theirs[h], mine[h])
        for b in (0, 1):
            for copy in axis_copies(mid, in1, one_ss, one_rs, kind, h, b, routes[b][0]):
                copy.start()

    def swap_two(kind, h):
        _, _, _, _, mid, in1, far, in2 = kinds[kind]
        for b in (0, 1):
            all_three(in1, one_rs, kind, h, b)
            far[h, b] = picked(mid, in1, h, b, routes[b][0])
            for copy in axis_copies(far, in2, two_ss, two_rs, kind, h, b, routes[b][1]):
                copy.start()

    def swapped(kind, h):
        _, _, _, _, _, _, far, in2 = kinds[kind]
        for b in (0, 1):
            all_three(in2, two_rs, kind, h, b)
        return [picked(far, in2, h, b, routes[b][1]) for b in (0, 1)]

    def tables():
        for s in range(1, SLOTS):

            @pl.when(me < s)
            def _():
                kvbuf[s] = jnp.zeros(kvbuf.shape[1:], kvbuf.dtype)
                posbuf[s] = jnp.full(posbuf.shape[1:], -1, jnp.int32)

        qpos = me * T + lax.broadcasted_iota(jnp.int32, (T, T), 0)
        start = jnp.zeros((T, T), jnp.int32)
        end = lens[0, 0]
        for k in range(1, 9):
            start = jnp.where(qpos >= end, jnp.maximum(start, end), start)
            if k < 8:
                end = end + lens[0, k]
        for s in range(SLOTS):
            if s > 0:

                @pl.when(me >= s)
                def _():
                    pos_copy(s).wait_recv()

            kpos = posbuf[s, 0:1, :]
            bias[:, s * T : (s + 1) * T] = jnp.where((kpos <= qpos) & (kpos >= start), 0.0, NEG)

        first = lax.broadcasted_iota(jnp.int32, (T, T), 0)
        second = lax.broadcasted_iota(jnp.int32, (T, T), 1)
        row = drow[...].astype(jnp.float32)
        column = jnp.sum(jnp.where(first == second, row, 0.0), axis=1, keepdims=True)
        same = (column == row) & (first < second)
        rank = jnp.sum(same.astype(jnp.int32), axis=0, keepdims=True)
        place = drow[...] * CAP + rank
        slot = lax.broadcasted_iota(jnp.int32, (N * CAP, T), 0)
        perm[...] = (slot == place).astype(jnp.float32).astype(jnp.bfloat16)

    def kv_copy(s, h, half):
        rows = slice(half * HALF, (half + 1) * HALF)
        return pltpu.make_async_remote_copy(
            src_ref=kvbuf.at[s, h, rows],
            dst_ref=kvbuf.at[s + 1, h, rows],
            send_sem=kv_ss.at[half, s, h],
            recv_sem=kv_rs.at[half, s + 1, h],
            device_id={"inner": lax.rem(me + 1, N)},
            device_id_type=MESH,
        )

    def pos_copy(s):
        return pltpu.make_async_remote_copy(
            src_ref=posbuf.at[0],
            dst_ref=posbuf.at[s],
            send_sem=pos_ss.at[s],
            recv_sem=pos_rs.at[s],
            device_id={"inner": lax.rem(me + s, N)},
            device_id_type=MESH,
        )

    def positions():
        lane = lax.broadcasted_iota(jnp.int32, posbuf.shape[1:], 1)
        part = lane // BLK
        block = jnp.where(
            part == 0, kept0, jnp.where(part == 1, kept1, jnp.where(part == 2, id0, id1))
        )
        posbuf[0] = me * T + block * BLK + lax.rem(lane, BLK)
        for s in range(1, SLOTS):

            @pl.when(me < N - s)
            def _():
                pos_copy(s).start()

    def row_copy(h, k):
        to = lax.rem(me + k, N)
        return pltpu.make_async_remote_copy(
            src_ref=sendbuf.at[h, to],
            dst_ref=recvbuf.at[h, me],
            send_sem=a_ss.at[h, k],
            recv_sem=a_rs.at[h, k],
            device_id={"inner": to},
            device_id_type=MESH,
        )

    def relay_in(h):
        return pltpu.make_async_remote_copy(
            src_ref=sendbuf.at[h, lax.rem(me + 4, N)],
            dst_ref=relay.at[h],
            send_sem=r_ss.at[0, h],
            recv_sem=r_rs.at[h],
            device_id={"inner": lax.rem(me + 6, N)},
            device_id_type=MESH,
        )

    def relay_out(h):
        return pltpu.make_async_remote_copy(
            src_ref=relay.at[h],
            dst_ref=recvbuf.at[h, lax.rem(me + 2, N)],
            send_sem=r_ss.at[1, h],
            recv_sem=a_rs.at[h, 4],
            device_id={"inner": lax.rem(me + 6, N)},
            device_id_type=MESH,
        )

    def pass_on(h):
        @pl.when(h < RELAYED)
        def _():
            relay_in(h).wait_recv()
            relay_out(h).start()

    def forward(s, h, half):
        if s > 0:

            @pl.when(me >= s)
            def _():
                kv_copy(s - 1, h, half).wait_recv()

        elif half == 0:
            cols = pl.ds(pl.multiple_of(h * 2 * D, D), 2 * D)
            kvbuf[0, h, :BLK, :] = one_block(kv, cols, kept0)
            kvbuf[0, h, BLK:HALF, :] = one_block(kv, cols, kept1)
        else:
            r0, r1 = swapped(0, h)
            kvbuf[0, h, HALF : HALF + BLK, :] = r0
            kvbuf[0, h, HALF + BLK :, :] = r1

        @pl.when((me >= s) & (me < N - 1))
        def _():
            kv_copy(s, h, half).start()

    factor = math.log2(math.e) / math.sqrt(D)

    def attend(h):
        @pl.when(me >= REACH)
        def _():
            for half in (0, 1):
                kv_copy(REACH - 1, h, half).wait_recv()

        own = q[:, pl.ds(pl.multiple_of(h * WQ, D), WQ)]
        r0, r1 = swapped(1, h)
        qh = jnp.concatenate(
            [chosen(b, own[b * BLK : (b + 1) * BLK], r0, r1) for b in range(T // BLK)], axis=0
        )
        keys = kvbuf[:, h, :, :D].reshape(KEYS, D)
        values = kvbuf[:, h, :, D:].reshape(KEYS, D)
        parts = []
        for g in range(PER):
            s = lax.dot_general(
                qh[:, g * D : (g + 1) * D],
                keys,
                (((1,), (1,)), ((), ())),
                preferred_element_type=jnp.float32,
            )
            s = s + bias[...]
            expo = jnp.exp2((s - jnp.max(s, axis=1, keepdims=True)) * factor)
            total = jnp.sum(expo, axis=1, keepdims=True)
            acc = jnp.dot(expo.astype(jnp.bfloat16), values, preferred_element_type=jnp.float32)
            parts.append((acc * (1.0 / total)).astype(jnp.bfloat16))
        attn = jnp.concatenate(parts, axis=1)
        placed = jnp.dot(perm[...], attn, preferred_element_type=jnp.float32)
        sendbuf[h] = placed.astype(jnp.bfloat16).reshape(N, CAP, WQ)
        recvbuf[h, me] = sendbuf[h, me]
        @pl.when(h < RELAYED)
        def _():
            relay_in(h).start()

        @pl.when(h >= RELAYED)
        def _():
            row_copy(h, 4).start()

        for k in DIRECT:
            row_copy(h, k).start()

    pl.semaphore_wait(barrier, len(greet))

    kv_lag = 3
    last = kv_lag + REACH
    stages = [(kv_lag + s, lambda h, s=s: forward(s, h, 1)) for s in reversed(range(REACH))]
    stages += [(2, lambda h: swap_two(0, h)), (1, lambda h: swap_one(0, h))]
    stages += [(0, lambda h: swap_core(0, h))]
    stages += [(s, lambda h, s=s: forward(s, h, 0)) for s in reversed(range(REACH))]
    stages += [(last - 1, lambda h: swap_two(1, h)), (last - 2, lambda h: swap_one(1, h))]
    stages += [(last - 3, lambda h: swap_core(1, h)), (last, attend)]
    stages = [(last + 1, pass_on)] + stages

    @pl.loop(0, KVH + last + 1)
    def _(t):
        for lag, stage in stages:
            h = t - lag

            @pl.when((h >= 0) & (h < KVH))
            def _():
                stage(h)

        @pl.when(t == 0)
        def _():
            positions()

        @pl.when(t == 3)
        def _():
            for load in loads[3:]:
                load.wait()
            tables()

    squares[...] = jnp.zeros_like(squares)

    @pl.loop(0, KVH)
    def _(h):
        for k in DIRECT:
            row_copy(h, k).wait_recv()
        relay_out(h).wait_recv()
        part = recvbuf[h].reshape(N * CAP, WQ).astype(jnp.float32)
        squares[...] = squares[...] + part * part

    @pl.loop(0, N)
    def _(i):
        rows = pl.ds(pl.multiple_of(i * CAP, CAP), CAP)
        mean = jnp.sum(squares[rows, :], axis=1, keepdims=True) * (1.0 / WIDTH)
        norm = lax.rsqrt(mean + 1e-06)
        for h in range(KVH):
            cols = slice(h * WQ, (h + 1) * WQ)
            part = recvbuf[h, i].astype(jnp.float32)
            out[rows, cols] = (part * norm * gain[:, cols]).astype(jnp.bfloat16)

    for s in range(1, SLOTS):

        @pl.when(me < N - s)
        def _():
            pos_copy(s).wait_send()

    @pl.loop(0, KVH)
    def _(h):
        for k in DIRECT:
            row_copy(h, k).wait_send()
        @pl.when(h < RELAYED)
        def _():
            relay_in(h).wait_send()
            relay_out(h).wait_send()

        @pl.when(h >= RELAYED)
        def _():
            row_copy(h, 4).wait_send()
        for s in range(REACH):

            @pl.when((me >= s) & (me < N - 1))
            def _():
                for half in (0, 1):
                    kv_copy(s, h, half).wait_send()

        for kind in (0, 1):
            core_copy(kind, h).wait_send()
            for b in (0, 1):
                all_three(kinds[kind][5], one_ss, kind, h, b)
                all_three(kinds[kind][7], two_ss, kind, h, b)


def shards(queries, key_values, doc_lengths, pairing, swap_ids, dest, gain):
    listed = swap_ids[0, 0]
    vmem = pl.BlockSpec(memory_space=pltpu.VMEM)
    hbm = pl.BlockSpec(memory_space=pltpu.HBM)
    dma = pltpu.SemaphoreType.DMA

    def swap_buffers(width):
        shapes = [(KVH, 2), (KVH, 2), (KVH, 2), (KVH, 2, 3), (KVH, 2), (KVH, 2, 3)]
        return [pltpu.VMEM((*shape, BLK, width), jnp.bfloat16) for shape in shapes]

    return pl.pallas_call(
        fused,
        name="attend_and_route",
        out_shape=jax.ShapeDtypeStruct((N * CAP, WIDTH), jnp.bfloat16),
        in_specs=[hbm] * 7,
        out_specs=vmem,
        scratch_shapes=[
            pltpu.SMEM((2,), jnp.int32),
            pltpu.SMEM((1, 8), jnp.int32),
            pltpu.SMEM((32,), jnp.int32),
            pltpu.VMEM((T, WIDTH), jnp.bfloat16),
            pltpu.VMEM((T, KVH * 2 * D), jnp.bfloat16),
            pltpu.VMEM((1, T), jnp.int32),
            pltpu.VMEM((1, WIDTH), jnp.float32),
            dma((7,)),
            pltpu.VMEM((SLOTS, KVH, T, 2 * D), jnp.bfloat16),
            pltpu.VMEM((SLOTS, 8, T), jnp.int32),
            pltpu.VMEM((KVH, N, CAP, WQ), jnp.bfloat16),
            pltpu.VMEM((KVH, N, CAP, WQ), jnp.bfloat16),
            pltpu.VMEM((KVH, CAP, WQ), jnp.bfloat16),
            pltpu.VMEM((N * CAP, WQ), jnp.float32),
            pltpu.VMEM((T, KEYS), jnp.float32),
            pltpu.VMEM((N * CAP, T), jnp.bfloat16),
            *swap_buffers(2 * D),
            *swap_buffers(WQ),
            *(dma((2, SLOTS, KVH)) for _ in range(2)),
            *(dma((SLOTS,)) for _ in range(2)),
            *(dma((KVH, N)) for _ in range(2)),
            dma((2, KVH)),
            dma((KVH,)),
            *(dma((2, KVH)) for _ in range(2)),
            *(dma((2, KVH, 2)) for _ in range(4)),
        ],
        compiler_params=pltpu.CompilerParams(
            collective_id=0, has_side_effects=True, vmem_limit_bytes=48 << 20
        ),
    )(
        *(
            pltpu.with_memory_space_constraint(a, pltpu.HBM)
            for a in (
                listed, doc_lengths, pairing, queries, key_values,
                dest.reshape(1, T), gain.reshape(1, WIDTH),
            )
        )
    )


def solution(mesh):
    return jax.shard_map(
        shards,
        mesh=mesh,
        in_specs=(
            P(("outer", "inner"), None),
            P(("outer", "inner"), None),
            P("outer", None),
            P(),
            P("outer", "inner", None),
            P(("outer", "inner"), None),
            P(),
        ),
        out_specs=P(("outer", "inner"), None),
        check_vma=False,
    )
```
